32 devices in a mesh: freq: 4 (over z), chan: 8 (over y, x, core).
Axes of the slice: x: 2, y: 2, z: 4, core: 2. Of those that a mesh axis runs over, the one named last changes fastest.
Arguments:
- raw_strain: bfloat16 [8, 32, 150000], P('chan', 'freq'), may hold values from -6 to 6
- fir_taps: bfloat16 [20], replicated, may hold values from -1.25 to 1.25
- band_bins: int32 [240], replicated, may hold values from 60 to 359, as said below
- live_mask: int32 [8, 32], P('chan', 'freq'), may hold values 0 or 1
Outputs:
- cross_spectra: float32 [240, 2, 256, 256], P('freq', None, 'chan')
The draws below stay inside these ranges and needn't reach their ends.
Inputs may be any that keep to these rules, and one draw needn't show every extreme that they name: `band_bins`: strictly increasing; the first is 60 and the last is 359.
All inputs are finite; a program needn't handle non-finite values. No bound on the sum of `live_mask` on one device may be relied on, other than what follows from the above.
Results may differ from the reference program's by a relative error of at most 0.0067.
Values may be sent and summed in bfloat16 or wider, within the bound.
No kernel may reach another device: no remote copies, remote signals or barrier semaphores. Data moves between devices by JAX's collectives and lax.ppermute only.
A program may use at most 64 MiB of HBM per device.

```python
import math
import jax
import jax.numpy as jnp
from jax import lax

CH_DEV = 32
C = 256
WIN = 10
DECIM = 10
TAPS = 20
NT = 1500
FB = 240
SPAN = 300
LOW = 60
N_CHAN = 8


def draw_band_bins(key, part):
    inner = SPAN - 2
    scores = jax.random.randint(key, (inner,), 0, 1000, dtype=jnp.int32) * inner + jnp.arange(inner, dtype=jnp.int32)
    values, picked = lax.top_k(scores, FB - 2)
    chosen = jnp.sort(picked.astype(jnp.int32)) + LOW + 1
    first = jnp.full((1,), LOW, dtype=jnp.int32)
    last = jnp.full((1,), LOW + SPAN - 1, dtype=jnp.int32)
    return jnp.concatenate([first, chosen, last]).astype(jnp.int32)


def set_ends(entries, own_key, low, largest):
    spot = [jax.random.randint(jax.random.fold_in(own_key, axis), (), 0, length) for axis, length in enumerate(entries.shape)]
    main_axis = entries.shape.index(max(entries.shape))
    beside = spot[:main_axis] + [(spot[main_axis] + 1) % entries.shape[main_axis]] + spot[main_axis + 1:]
    return entries.at[tuple(spot)].set(low).at[tuple(beside)].set(largest)


def block_scale(stream_key, extent, pieces, smallest, high):
    def one(axis_at, parts):
        heights = jax.random.uniform(jax.random.fold_in(jax.random.fold_in(stream_key, 6), axis_at), (parts,), jnp.float32, smallest / len(pieces), high / len(pieces))
        return jnp.repeat(jnp.exp(heights), extent[axis_at] // parts).reshape((-1,) + (1,) * (len(extent) - axis_at - 1))

    loudness = one(*pieces[0])
    for cut in pieces[1:]:
        loudness = loudness * one(*cut)
    return loudness


def gaussian(stream_key, shape, spread, limit, shards=(), held_as=jnp.bfloat16):
    array = spread * jax.random.normal(stream_key, shape, jnp.float32)
    if shards:
        array = array * block_scale(stream_key, shape, shards, -0.22, 0.18)
    return jnp.clip(array, -limit, limit).astype(held_as)


def setup_inputs(seed: int = 0) -> dict:
    streams_of = jax.random.split(jax.random.key(seed), 5)
    raw_strain = gaussian(streams_of[0], (N_CHAN, CH_DEV, WIN * NT * DECIM), 1.0, 6.0, ((0, 8), (1, 4)))
    fir_taps = gaussian(streams_of[1], (TAPS,), TAPS ** -0.5, 1.25)
    band_bins = draw_band_bins(jax.random.fold_in(streams_of[4], 71), 0)
    live_mask = set_ends((jax.random.randint(streams_of[3], (N_CHAN, CH_DEV), 0, 10) < 9).astype(jnp.int32), jax.random.fold_in(streams_of[3], 1), 0, 1)
    return dict(raw_strain=raw_strain, fir_taps=fir_taps, band_bins=band_bins, live_mask=live_mask)


def make_table(band_bins):
    times = jnp.arange(NT, dtype=jnp.int32)[:, None]
    phase = times * band_bins[None, :].astype(jnp.int32) % NT
    angle = phase.astype(jnp.float32) * jnp.float32(2.0 * math.pi / NT)
    return jnp.concatenate([jnp.cos(angle), -jnp.sin(angle)], axis=1).astype(jnp.bfloat16)

def prepare(block, fir_taps, table, mask_row):
    rows = block.shape[0]
    samples = block.reshape(rows * WIN * NT, DECIM)
    tap_cols = jnp.transpose(fir_taps.reshape(2, DECIM)[:, ::-1])
    part = jnp.dot(samples, tap_cols, preferred_element_type=jnp.float32).reshape(rows, WIN, NT, 2)
    previous = jnp.pad(part[..., 1], ((0, 0), (0, 0), (1, 0)))[..., :NT]
    decimated = (part[..., 0] + previous).astype(jnp.bfloat16)
    spectrum = jnp.dot(decimated.reshape(rows * WIN, NT), table, preferred_element_type=jnp.float32)
    spectrum = spectrum.reshape(rows, WIN, 2, FB)
    power = lax.optimization_barrier(jnp.sum(spectrum * spectrum, axis=(2, 3))) / FB
    scale = lax.rsqrt(power + 1e-06) * mask_row.astype(jnp.float32)[:, None]
    return (spectrum * scale[:, :, None, None]).astype(jnp.bfloat16)

def reference(raw_strain, fir_taps, band_bins, live_mask):
    table = make_table(band_bins)

    def one_block(pair):
        block, mask_row = pair
        return prepare(block, fir_taps, table, mask_row)
    whitened = lax.map(one_block, (raw_strain, live_mask))
    whitened = whitened.reshape(C, WIN, 2, FB)
    ordered = jnp.transpose(whitened, (3, 2, 1, 0))

    def one_bin(spec):
        spec32 = spec.astype(jnp.float32)
        prod = jnp.einsum('awi,bwj->abij', spec32, spec32)
        real_part = prod[0, 0] + prod[1, 1]
        imag_part = prod[1, 0] - prod[0, 1]
        return jnp.stack([real_part, imag_part], axis=0) / WIN
    return lax.map(one_bin, ordered)
```

```python
import functools
import math

import jax
import jax.numpy as jnp
from jax import lax
from jax.experimental import pallas as pl
from jax.experimental.pallas import tpu as pltpu
from jax.sharding import PartitionSpec as P

WIN = 10
DECIM = 10
NT = 1500
LANES = 128
SUB = 8
F32 = jnp.float32
BF16 = jnp.bfloat16


def up(value, unit):
    return -(-value // unit) * unit


def iota(shape, axis):
    return lax.broadcasted_iota(jnp.int32, shape, axis)


def wrap(product, length):
    turns = jnp.floor((product.astype(F32) + 0.5) * F32(1.0 / length)).astype(jnp.int32)
    return product - turns * length


def cos_sin(phase, length):
    four = 4 * phase
    quad = jnp.floor((four.astype(F32) + (0.5 * length + 0.5)) * F32(1.0 / length)).astype(jnp.int32)
    angle = (four - quad * length).astype(F32) * F32(2.0 * math.pi / (4 * length))
    sq = angle * angle
    sin = angle * (1.0 + sq * (F32(-1 / 6) + sq * (F32(1 / 120) + sq * (F32(-1 / 5040) + sq * F32(1 / 362880)))))
    cos = 1.0 + sq * (F32(-0.5) + sq * (F32(1 / 24) + sq * (F32(-1 / 720) + sq * (F32(1 / 40320) + sq * F32(-1 / 3628800)))))
    odd = (quad & 1) == 1
    c0 = jnp.where(odd, sin, cos)
    s0 = jnp.where(odd, cos, sin)
    c = jnp.where(((quad + 1) & 2) == 2, -c0, c0)
    s = jnp.where((quad & 2) == 2, -s0, s0)
    return c, s


def front_kernel(dims, mask_ref, x_hbm, taps_ref, bins_ref, *refs):
    windows, length, factor, groups, per_group, half, rows = dims
    outs = refs[:groups]
    x_ref, band_ref, table_ref, lhs_ref, dec_ref, sem = refs[groups:]
    copy = pltpu.make_async_copy(x_hbm.at[0], x_ref, sem)
    copy.start()
    width = groups * 2 * half
    chunk = factor * LANES
    tiles = factor + 1
    tap_count = taps_ref.shape[1]

    taps = jnp.concatenate([taps_ref[...].astype(F32), jnp.zeros((1, LANES - tap_count), F32)], axis=1)
    taps = jnp.broadcast_to(taps, (SUB, LANES))
    base = factor * iota((SUB, LANES), 1) + (factor - 1 + LANES) - iota((SUB, LANES), 0)
    for row in range(0, tiles * LANES, 2 * SUB):
        pair = []
        for start in (row, row + SUB):
            tap = base - start
            tap = jnp.where((tap >= 0) & (tap < tap_count), tap, LANES - 1)
            pair.append(jnp.take_along_axis(taps, tap, axis=1, mode="promise_in_bounds"))
        band_ref[row : row + 2 * SUB, :] = jnp.concatenate(pair, axis=0).astype(BF16)

    own = lax.axis_index("freq")
    bin_count = bins_ref.shape[1]
    held = up(bin_count, LANES)
    bins = bins_ref[...]
    if held > bin_count:
        bins = jnp.concatenate([bins, jnp.zeros((1, held - bin_count), jnp.int32)], axis=1)
    bins = jnp.broadcast_to(bins, (SUB, held))
    lane = iota((SUB, 2 * half), 1)
    is_imag = lane >= half
    columns = []
    for slot in range(groups):
        first = (own ^ slot) * per_group
        real = pltpu.roll(bins, lax.rem(held - first, held), 1)[:, : 2 * half]
        imag = pltpu.roll(bins, lax.rem(held - first + half, held), 1)[:, : 2 * half]
        columns.append(jnp.where(is_imag, imag, real))
    blocks = up(length, LANES) // LANES
    steps = iota((up(blocks, SUB), 2 * half), 0)
    valid = (lane & (half - 1)) < per_group
    for slot in range(groups):
        bins8 = columns[slot]
        turn_rows = [
            cos_sin(wrap((steps[r : r + SUB] * LANES) * bins8, length), length)
            for r in range(0, steps.shape[0], SUB)
        ]
        for row in range(0, LANES, 2 * SUB):
            here = []
            for start in (row, row + SUB):
                c, s = cos_sin(wrap((iota((SUB, 2 * half), 0) + start) * bins8, length), length)
                here.append((
                    jnp.where(valid, jnp.where(is_imag, -s, c), 0.0),
                    jnp.where(valid, jnp.where(is_imag, -c, -s), 0.0),
                ))
            for block in range(blocks):
                turn_c, turn_s = turn_rows[block // SUB]
                at = block % SUB
                turn_c, turn_s = turn_c[at : at + 1], turn_s[at : at + 1]
                value = [v * turn_c + w * turn_s for v, w in here]
                table_ref[
                    block * LANES + row : block * LANES + row + 2 * SUB,
                    slot * 2 * half : (slot + 1) * 2 * half,
                ] = jnp.concatenate(value, axis=0).astype(BF16)

    copy.wait()
    total = x_ref.shape[1]
    chunks = -(-total // chunk)
    entries = [(q, 0) for q in range(chunks)]
    for w in range(1, windows):
        begin = w * length * factor
        entries.append((begin // chunk, begin))
    zero_tile = jnp.zeros((rows, LANES), F32)
    lane8 = iota((rows, LANES), 1)

    def tile_of(entry, tile):
        q, begin = entry
        start = q * chunk + (tile - 1) * LANES
        if start < 0 or start >= total or start + LANES <= begin:
            return zero_tile
        stop = min(start + LANES, total)
        got = x_ref[:, start:stop].astype(F32)
        if stop - start < LANES:
            got = jnp.concatenate([got, jnp.zeros((rows, LANES - (stop - start)), F32)], axis=1)
        if start < begin:
            got = jnp.where(lane8 >= begin - start, got, 0.0)
        return got

    if len(entries) % 2:
        entries.append((chunks, 0))
    for pair in range(0, len(entries), 2):
        for tile in range(tiles):
            both = [tile_of(entries[pair + e], tile) for e in range(2)]
            lhs_ref[pair * rows : (pair + 2) * rows, tile * LANES : (tile + 1) * LANES] = (
                jnp.concatenate(both, axis=0).astype(BF16)
            )
    dec_ref[...] = jnp.dot(lhs_ref[:, 0 : tiles * LANES], band_ref[...], preferred_element_type=F32)

    def dec(entry):
        return dec_ref[entry * rows : (entry + 1) * rows, :]

    spectrum = None
    for block in range(blocks):
        parts = []
        for w in range(windows):
            first, lead = divmod(w * length, LANES)
            entry = first + block
            low = dec(chunks + w - 1) if (block == 0 and w > 0) else dec(entry)
            if lead:
                low = pltpu.roll(low, LANES - lead, 1)
                if entry + 1 < chunks:
                    high = pltpu.roll(dec(entry + 1), LANES - lead, 1)
                    low = jnp.where(lane8 < LANES - lead, low, high)
            left = length - block * LANES
            if left < LANES:
                low = jnp.where(lane8 < left, low, 0.0)
            parts.append(low)
        lhs = jnp.concatenate(parts, axis=0).astype(BF16)
        lhs_ref[0 : windows * rows, block * LANES : (block + 1) * LANES] = lhs
    spectrum = jnp.dot(
        lhs_ref[0 : windows * rows, 0 : blocks * LANES], table_ref[...], preferred_element_type=F32
    )
    power = jnp.sum(spectrum * spectrum, axis=1, keepdims=True) / bin_count
    row = iota((windows * rows, 1), 0) & (rows - 1)
    live = jnp.zeros((windows * rows, 1), F32)
    for r in range(rows):
        live = jnp.where(row == r, mask_ref[0, r].astype(F32), live)
    scale = lax.rsqrt(power + 1e-06) * live
    for slot in range(groups):
        piece = spectrum[:, slot * 2 * half : (slot + 1) * 2 * half] * scale
        outs[slot][...] = piece.astype(BF16)


def front(raw_strain, fir_taps, band_bins, live_mask, groups):
    rows = raw_strain.shape[1]
    bins = band_bins.shape[0]
    per_group = bins // groups
    half = up(per_group, 64)
    dims = (WIN, NT, DECIM, groups, per_group, half, rows)
    width = groups * 2 * half
    total = raw_strain.shape[2]
    chunks = -(-total // (DECIM * LANES))
    entries = up(chunks + WIN - 1, 2)
    blocks = up(NT, LANES)
    vmem = pl.BlockSpec(memory_space=pltpu.VMEM)
    return pl.pallas_call(
        functools.partial(front_kernel, dims),
        out_shape=[jax.ShapeDtypeStruct((WIN * rows, 2 * half), BF16)] * groups,
        in_specs=[
            pl.BlockSpec(memory_space=pltpu.SMEM),
            pl.BlockSpec(memory_space=pltpu.HBM),
            vmem,
            vmem,
        ],
        out_specs=[vmem] * groups,
        scratch_shapes=[
            pltpu.VMEM((rows, total), BF16),
            pltpu.VMEM(((DECIM + 1) * LANES, LANES), BF16),
            pltpu.VMEM((blocks, width), BF16),
            pltpu.VMEM((entries * rows, max((DECIM + 1) * LANES, blocks)), BF16),
            pltpu.VMEM((entries * rows, LANES), F32),
            pltpu.SemaphoreType.DMA,
        ],
        compiler_params=pltpu.CompilerParams(vmem_limit_bytes=20 << 20),
        name="front",
    )(live_mask, raw_strain, fir_taps[None, :], band_bins[None, :])


def correlate_kernel(dims, step_bins, parts_ref, out_ref, *spec_refs):
    windows, rows, zs, blocks, half = dims
    height = rows * zs
    width = height * blocks
    block = lax.axis_index("chan")
    z_own = lax.axis_index("freq")

    @pl.when(pl.program_id(0) == 0)
    def _():
        lane = iota((height, 2 * half), 1)
        for pair in range(0, windows, 2):
            at = pair * rows
            slabs = ([], [])
            for b in range(blocks):
                for z in range(zs):
                    got = parts_ref[block ^ b, z_own ^ z, at : at + 2 * rows, :].astype(F32)
                    slabs[0].append(got[:rows])
                    slabs[1].append(got[rows:])
            mine = ([], [])
            for z in range(zs):
                got = parts_ref[0, z_own ^ z, at : at + 2 * rows, :].astype(F32)
                mine[0].append(got[:rows])
                mine[1].append(got[rows:])
            for e in range(2):
                own = jnp.concatenate(mine[e], axis=0)
                turned = jnp.where(lane < half, pltpu.roll(own, half, 1), -pltpu.roll(own, half, 1))
                tail = jnp.zeros((up(2 * height, LANES) - 2 * height, 2 * half), F32)
                full = jnp.concatenate(slabs[e] + [own, turned, tail], axis=0)
                start = 2 * half * (pair + e)
                for r in range(0, full.shape[0], LANES):
                    spec_refs[r // LANES][start : start + 2 * half, :] = full[r : r + LANES].T

    first = pl.program_id(0) * step_bins
    for k in range(step_bins):
        got = [ref[pl.ds(first + k, 2 * windows, stride=half), :] for ref in spec_refs]
        got = jnp.concatenate(got, axis=1).astype(BF16)
        prod = lax.dot_general(
            got[:, width : width + 2 * height], got[:, :width],
            (((0,), (0,)), ((), ())), preferred_element_type=F32,
        ) * F32(1.0 / windows)
        out_ref[k, 0] = prod[:height]
        out_ref[k, 1] = prod[height:]


def correlate(parts, per_group, rows):
    blocks, zs, full_rows, lanes = parts.shape
    windows = full_rows // rows
    half = lanes // 2
    height = rows * zs
    width = height * blocks
    step_bins = next(s for s in (10, 6, 5, 4, 3, 2, 1) if per_group % s == 0)
    dims = (windows, rows, zs, blocks, half)
    return pl.pallas_call(
        functools.partial(correlate_kernel, dims, step_bins),
        grid=(per_group // step_bins,),
        out_shape=jax.ShapeDtypeStruct((per_group, 2, height, width), F32),
        in_specs=[pl.BlockSpec(memory_space=pltpu.VMEM)],
        out_specs=pl.BlockSpec((step_bins, 2, height, width), lambda i: (i, 0, 0, 0)),
        scratch_shapes=[pltpu.VMEM((windows * 2 * half, LANES), F32)]
        * ((width + up(2 * height, LANES)) // LANES),
        compiler_params=pltpu.CompilerParams(vmem_limit_bytes=16 << 20),
        name="correlate",
    )(parts)


def shards(groups, blocks, raw_strain, fir_taps, band_bins, live_mask):
    rows = raw_strain.shape[1]
    per_group = band_bins.shape[0] // groups
    pieces = front(raw_strain, fir_taps, band_bins, live_mask, groups)
    got = [pieces[0]]
    for slot in range(groups - 1, 0, -1):
        pairs = [(i, i ^ slot) for i in range(groups)]
        got.insert(1, lax.ppermute(pieces[slot], "freq", pairs))
    parts = jnp.stack(got)[None]
    step = 2
    order = []
    while step < blocks:
        order.append(step)
        step *= 2
    order.append(1)
    slots = [0]
    held = {0: parts}
    for step in order:
        base = jnp.concatenate([held[s] for s in slots], axis=0) if len(slots) > 1 else held[slots[0]]
        moved = lax.ppermute(base, "chan", [(i, i ^ step) for i in range(blocks)])
        for n, s in enumerate(list(slots)):
            held[s ^ step] = moved[n : n + 1]
            slots.append(s ^ step)
    parts = jnp.concatenate([held[s] for s in range(blocks)], axis=0)
    return correlate(parts, per_group, rows)


def solution(mesh):
    in_specs = (P("chan", "freq", None), P(), P(), P("chan", "freq"))
    out_specs = P("freq", None, "chan", None)
    body = functools.partial(shards, mesh.shape["freq"], mesh.shape["chan"])
    return jax.shard_map(body, mesh=mesh, in_specs=in_specs, out_specs=out_specs, check_vma=False)
```

```python
import functools
import math

import jax
import jax.numpy as jnp
from jax import lax
from jax.experimental import pallas as pl
from jax.experimental.pallas import tpu as pltpu
from jax.sharding import PartitionSpec as P

WIN = 10
DECIM = 10
NT = 1500
LANES = 128
SUB = 8
F32 = jnp.float32
BF16 = jnp.bfloat16


def up(value, unit):
    return -(-value // unit) * unit


def iota(shape, axis):
    return lax.broadcasted_iota(jnp.int32, shape, axis)


def wrap(product, length):
    turns = jnp.floor((product.astype(F32) + 0.5) * F32(1.0 / length)).astype(jnp.int32)
    return product - turns * length


def cos_sin(phase, length):
    four = 4 * phase
    quad = jnp.floor((four.astype(F32) + (0.5 * length + 0.5)) * F32(1.0 / length)).astype(jnp.int32)
    angle = (four - quad * length).astype(F32) * F32(2.0 * math.pi / (4 * length))
    sq = angle * angle
    sin = angle * (1.0 + sq * (F32(-1 / 6) + sq * (F32(1 / 120) + sq * (F32(-1 / 5040) + sq * F32(1 / 362880)))))
    cos = 1.0 + sq * (F32(-0.5) + sq * (F32(1 / 24) + sq * (F32(-1 / 720) + sq * (F32(1 / 40320) + sq * F32(-1 / 3628800)))))
    odd = (quad & 1) == 1
    c0 = jnp.where(odd, sin, cos)
    s0 = jnp.where(odd, cos, sin)
    c = jnp.where(((quad + 1) & 2) == 2, -c0, c0)
    s = jnp.where((quad & 2) == 2, -s0, s0)
    return c, s


def front_kernel(dims, mask_hbm, x_hbm, taps_hbm, bins_hbm, *refs):
    windows, length, factor, groups, per_group, half, rows = dims
    outs = refs[:groups]
    x_ref, mask_ref, taps_ref, bins_ref, band_ref, table_ref, lhs_ref, dec_ref, sems = refs[groups:]
    small = [
        pltpu.make_async_copy(src, dst, sems.at[n])
        for n, (src, dst) in enumerate(((taps_hbm, taps_ref), (bins_hbm, bins_ref), (mask_hbm, mask_ref)))
    ]
    for each in small:
        each.start()
    copy = pltpu.make_async_copy(x_hbm.at[0], x_ref, sems.at[3])
    copy.start()
    for each in small:
        each.wait()
    width = groups * 2 * half
    chunk = factor * LANES
    tiles = factor + 1
    tap_count = taps_ref.shape[1]

    taps = jnp.concatenate([taps_ref[...].astype(F32), jnp.zeros((1, LANES - tap_count), F32)], axis=1)
    taps = jnp.broadcast_to(taps, (SUB, LANES))
    base = factor * iota((SUB, LANES), 1) + (factor - 1 + LANES) - iota((SUB, LANES), 0)
    for row in range(0, tiles * LANES, 2 * SUB):
        pair = []
        for start in (row, row + SUB):
            tap = base - start
            tap = jnp.where((tap >= 0) & (tap < tap_count), tap, LANES - 1)
            pair.append(jnp.take_along_axis(taps, tap, axis=1, mode="promise_in_bounds"))
        band_ref[row : row + 2 * SUB, :] = jnp.concatenate(pair, axis=0).astype(BF16)

    own = lax.axis_index("freq")
    bin_count = bins_ref.shape[1]
    held = up(bin_count, LANES)
    bins = bins_ref[...]
    if held > bin_count:
        bins = jnp.concatenate([bins, jnp.zeros((1, held - bin_count), jnp.int32)], axis=1)
    bins = jnp.broadcast_to(bins, (SUB, held))
    lane = iota((SUB, 2 * half), 1)
    is_imag = lane >= half
    columns = []
    for slot in range(groups):
        first = lax.rem(own + slot, groups) * per_group
        real = pltpu.roll(bins, lax.rem(held - first, held), 1)[:, : 2 * half]
        imag = pltpu.roll(bins, lax.rem(held - first + half, held), 1)[:, : 2 * half]
        columns.append(jnp.where(is_imag, imag, real))
    blocks = up(length, LANES) // LANES
    steps = iota((up(blocks, SUB), 2 * half), 0)
    valid = (lane & (half - 1)) < per_group
    for slot in range(groups):
        bins8 = columns[slot]
        turn_rows = [
            cos_sin(wrap((steps[r : r + SUB] * LANES) * bins8, length), length)
            for r in range(0, steps.shape[0], SUB)
        ]
        for row in range(0, LANES, 2 * SUB):
            here = []
            for start in (row, row + SUB):
                c, s = cos_sin(wrap((iota((SUB, 2 * half), 0) + start) * bins8, length), length)
                here.append((
                    jnp.where(valid, jnp.where(is_imag, -s, c), 0.0),
                    jnp.where(valid, jnp.where(is_imag, -c, -s), 0.0),
                ))
            for block in range(blocks):
                turn_c, turn_s = turn_rows[block // SUB]
                at = block % SUB
                turn_c, turn_s = turn_c[at : at + 1], turn_s[at : at + 1]
                value = [v * turn_c + w * turn_s for v, w in here]
                table_ref[
                    block * LANES + row : block * LANES + row + 2 * SUB,
                    slot * 2 * half : (slot + 1) * 2 * half,
                ] = jnp.concatenate(value, axis=0).astype(BF16)

    copy.wait()
    total = x_ref.shape[1]
    chunks = -(-total // chunk)
    entries = [(q, 0) for q in range(chunks)]
    for w in range(1, windows):
        begin = w * length * factor
        entries.append((begin // chunk, begin))
    zero_tile = jnp.zeros((rows, LANES), F32)
    lane8 = iota((rows, LANES), 1)

    def tile_of(entry, tile):
        q, begin = entry
        start = q * chunk + (tile - 1) * LANES
        if start < 0 or start >= total or start + LANES <= begin:
            return zero_tile
        stop = min(start + LANES, total)
        got = x_ref[:, start:stop].astype(F32)
        if stop - start < LANES:
            got = jnp.concatenate([got, jnp.zeros((rows, LANES - (stop - start)), F32)], axis=1)
        if start < begin:
            got = jnp.where(lane8 >= begin - start, got, 0.0)
        return got

    if len(entries) % 2:
        entries.append((chunks, 0))
    for pair in range(0, len(entries), 2):
        for tile in range(tiles):
            both = [tile_of(entries[pair + e], tile) for e in range(2)]
            lhs_ref[pair * rows : (pair + 2) * rows, tile * LANES : (tile + 1) * LANES] = (
                jnp.concatenate(both, axis=0).astype(BF16)
            )
    dec_ref[...] = jnp.dot(lhs_ref[:, 0 : tiles * LANES], band_ref[...], preferred_element_type=F32)

    def dec(entry):
        return dec_ref[entry * rows : (entry + 1) * rows, :]

    spectrum = None
    for block in range(blocks):
        parts = []
        for w in range(windows):
            first, lead = divmod(w * length, LANES)
            entry = first + block
            low = dec(chunks + w - 1) if (block == 0 and w > 0) else dec(entry)
            if lead:
                low = pltpu.roll(low, LANES - lead, 1)
                if entry + 1 < chunks:
                    high = pltpu.roll(dec(entry + 1), LANES - lead, 1)
                    low = jnp.where(lane8 < LANES - lead, low, high)
            left = length - block * LANES
            if left < LANES:
                low = jnp.where(lane8 < left, low, 0.0)
            parts.append(low)
        lhs = jnp.concatenate(parts, axis=0).astype(BF16)
        lhs_ref[0 : windows * rows, block * LANES : (block + 1) * LANES] = lhs
    spectrum = jnp.dot(
        lhs_ref[0 : windows * rows, 0 : blocks * LANES], table_ref[...], preferred_element_type=F32
    )
    power = jnp.sum(spectrum * spectrum, axis=1, keepdims=True) / bin_count
    row = iota((windows * rows, 1), 0) & (rows - 1)
    live = jnp.zeros((windows * rows, 1), F32)
    for r in range(rows):
        live = jnp.where(row == r, mask_ref[0, r].astype(F32), live)
    scale = lax.rsqrt(power + 1e-06) * live
    for slot in range(groups):
        piece = spectrum[:, slot * 2 * half : (slot + 1) * 2 * half] * scale
        outs[slot][...] = piece.astype(BF16)


def front(raw_strain, fir_taps, band_bins, live_mask, groups):
    rows = raw_strain.shape[1]
    bins = band_bins.shape[0]
    per_group = bins // groups
    half = up(per_group, 64)
    dims = (WIN, NT, DECIM, groups, per_group, half, rows)
    width = groups * 2 * half
    total = raw_strain.shape[2]
    chunks = -(-total // (DECIM * LANES))
    entries = up(chunks + WIN - 1, 2)
    blocks = up(NT, LANES)
    vmem = pl.BlockSpec(memory_space=pltpu.VMEM)
    return pl.pallas_call(
        functools.partial(front_kernel, dims),
        out_shape=[jax.ShapeDtypeStruct((WIN * rows, 2 * half), BF16)] * groups,
        in_specs=[pl.BlockSpec(memory_space=pltpu.HBM)] * 4,
        out_specs=[vmem] * groups,
        scratch_shapes=[
            pltpu.VMEM((rows, total), BF16),
            pltpu.SMEM(live_mask.shape, jnp.int32),
            pltpu.VMEM((1, fir_taps.shape[0]), BF16),
            pltpu.VMEM((1, bins), jnp.int32),
            pltpu.VMEM(((DECIM + 1) * LANES, LANES), BF16),
            pltpu.VMEM((blocks, width), BF16),
            pltpu.VMEM((entries * rows, max((DECIM + 1) * LANES, blocks)), BF16),
            pltpu.VMEM((entries * rows, LANES), F32),
            pltpu.SemaphoreType.DMA((4,)),
        ],
        compiler_params=pltpu.CompilerParams(vmem_limit_bytes=20 << 20),
        name="front",
    )(*[
        pltpu.with_memory_space_constraint(a, pltpu.HBM)
        for a in (live_mask, raw_strain, fir_taps[None, :], band_bins[None, :])
    ])


def rows_kernel(dims, parts_ref, out_ref, turned_ref):
    windows, rows, zs, half, per_group, pack = dims
    height = rows * zs
    own = lax.axis_index("freq")
    lane = iota((height, 2 * half), 1)
    depth = 2 * windows
    blank = jnp.zeros((LANES - 2 * height, 2 * half), F32)
    for pair in range(0, windows, 2):
        mine = ([], [])
        for z in range(zs):
            slot = lax.rem(own + zs - z, zs)
            got = parts_ref[slot, pair * rows : (pair + 2) * rows, :].astype(F32)
            mine[0].append(got[:rows])
            mine[1].append(got[rows:])
        for e in range(2):
            straight = jnp.concatenate(mine[e], axis=0)
            swapped = pltpu.roll(straight, half, 1)
            swapped = jnp.where(lane < half, swapped, -swapped)
            flipped = jnp.concatenate([straight, swapped, blank], axis=0).T
            for part in range(2):
                turned_ref[pl.ds(2 * (pair + e) + part, half, stride=depth), :] = flipped[part * half : (part + 1) * half]
    lane = iota((2 * height, LANES), 1)
    for group in range(per_group // pack):
        got = turned_ref[group * pack * depth : (group + 1) * pack * depth, :]
        got = jnp.concatenate([got, jnp.zeros((LANES - pack * depth, LANES), F32)], axis=0).T[: 2 * height]
        for k in range(pack):
            inside = (lane >= k * depth) & (lane < (k + 1) * depth)
            out_ref[group, k * 2 * height : (k + 1) * 2 * height, :] = jnp.where(inside, got, 0.0).astype(BF16)


def correlate_kernel(dims, left_ref, parts_ref, out_hbm, *refs):
    windows, rows, zs, blocks, half, per_group, pack = dims
    *spec_refs, out_ref, sems = refs
    height = rows * zs
    depth = 2 * windows
    block = lax.axis_index("chan")
    own = lax.axis_index("freq")
    per_tile = LANES // height
    for pair in range(0, windows, 2):
        for tile, spec_ref in enumerate(spec_refs):
            slabs = ([], [])
            for b in range(tile * per_tile, (tile + 1) * per_tile):
                for z in range(zs):
                    slot = lax.rem(own + zs - z, zs)
                    got = parts_ref[(block ^ b) & 1, (block ^ b) >> 1, slot, pair * rows : (pair + 2) * rows, :].astype(F32)
                    slabs[0].append(got[:rows])
                    slabs[1].append(got[rows:])
            for e in range(2):
                flipped = jnp.concatenate(slabs[e], axis=0).T
                for part in range(2):
                    spec_ref[pl.ds(2 * (pair + e) + part, half, stride=depth), :] = flipped[part * half : (part + 1) * half]
    copies = []
    for group in range(per_group // pack):
        at = group * pack * depth
        right = [ref[at : at + pack * depth, :] for ref in spec_refs]
        right = jnp.concatenate(right, axis=1).astype(BF16)
        prod = jnp.dot(left_ref[group, :, : pack * depth], right, preferred_element_type=F32)
        prod = prod * F32(1.0 / windows)
        first = group * pack
        out_ref[first : first + pack] = prod.reshape(pack, 2, height, prod.shape[1])
        copies.append(pltpu.make_async_copy(out_ref.at[pl.ds(first, pack)], out_hbm.at[pl.ds(first, pack)], sems.at[group]))
        copies[-1].start()
    for each in copies:
        each.wait()


def pack_of(per_group, windows):
    return next(p for p in (4, 2, 1) if per_group % p == 0 and 2 * windows * p <= LANES)


def row_side(parts, per_group, rows):
    zs, full_rows, lanes = parts.shape
    windows = full_rows // rows
    pack = pack_of(per_group, windows)
    half = lanes // 2
    height = rows * zs
    vmem = pl.BlockSpec(memory_space=pltpu.VMEM)
    return pl.pallas_call(
        functools.partial(rows_kernel, (windows, rows, zs, half, per_group, pack)),
        out_shape=jax.ShapeDtypeStruct((per_group // pack, pack * 2 * height, LANES), BF16),
        in_specs=[vmem],
        out_specs=vmem,
        scratch_shapes=[pltpu.VMEM((half * 2 * windows, LANES), F32)],
        compiler_params=pltpu.CompilerParams(vmem_limit_bytes=8 << 20),
        cost_estimate=pl.CostEstimate(flops=1 << 24, bytes_accessed=4 << 20, transcendentals=0),
        name="rows",
    )(parts)


def correlate(left, parts, per_group, rows):
    _, chips, zs, full_rows, lanes = parts.shape
    blocks = 2 * chips
    windows = full_rows // rows
    half = lanes // 2
    height = rows * zs
    width = height * blocks
    pack = pack_of(per_group, windows)
    dims = (windows, rows, zs, blocks, half, per_group, pack)
    vmem = pl.BlockSpec(memory_space=pltpu.VMEM)
    shape = (per_group, 2, height, width)
    return pl.pallas_call(
        functools.partial(correlate_kernel, dims),
        out_shape=jax.ShapeDtypeStruct(shape, F32),
        in_specs=[vmem, vmem],
        out_specs=pl.BlockSpec(memory_space=pltpu.HBM),
        scratch_shapes=[pltpu.VMEM((half * 2 * windows, LANES), F32)] * (width // LANES)
        + [pltpu.VMEM(shape, F32), pltpu.SemaphoreType.DMA((per_group // pack,))],
        compiler_params=pltpu.CompilerParams(vmem_limit_bytes=(24 if blocks <= 8 else 44) << 20),
        name="correlate",
    )(left, parts)


def shards(groups, blocks, raw_strain, fir_taps, band_bins, live_mask):
    rows = raw_strain.shape[1]
    per_group = band_bins.shape[0] // groups
    pieces = front(raw_strain, fir_taps, band_bins, live_mask, groups)
    got = [pieces[0]]
    for slot in range(1, groups):
        pairs = [(i, (i + slot) % groups) for i in range(groups)]
        got.append(lax.ppermute(pieces[slot], "freq", pairs))
    parts = jnp.stack(got)
    left = row_side(parts, per_group, rows)
    same = [parts[None]]
    for step in range(2, blocks, 2):
        same.append(lax.ppermute(parts[None], "chan", [(i, i ^ step) for i in range(blocks)]))
    same = jnp.concatenate(same, axis=0)
    other = lax.ppermute(same, "chan", [(i, i ^ 1) for i in range(blocks)])
    both = jnp.stack([same, other])
    return correlate(left, both, per_group, rows)


def solution(mesh):
    in_specs = (P("chan", "freq", None), P(), P(), P("chan", "freq"))
    out_specs = P("freq", None, "chan", None)
    body = functools.partial(shards, mesh.shape["freq"], mesh.shape["chan"])
    return jax.shard_map(body, mesh=mesh, in_specs=in_specs, out_specs=out_specs, check_vma=False)
```

```python
import functools
import math

import jax
import jax.numpy as jnp
from jax import lax
from jax.experimental import pallas as pl
from jax.experimental.pallas import tpu as pltpu
from jax.sharding import PartitionSpec as P

WIN = 10
DECIM = 10
NT = 1500
LANES = 128
SUB = 8
F32 = jnp.float32
BF16 = jnp.bfloat16


def up(value, unit):
    return -(-value // unit) * unit


def iota(shape, axis):
    return lax.broadcasted_iota(jnp.int32, shape, axis)


def wrap(product, length):
    turns = jnp.floor((product.astype(F32) + 0.5) * F32(1.0 / length)).astype(jnp.int32)
    return product - turns * length


def cos_sin(phase, length):
    four = 4 * phase
    quad = jnp.floor((four.astype(F32) + (0.5 * length + 0.5)) * F32(1.0 / length)).astype(jnp.int32)
    angle = (four - quad * length).astype(F32) * F32(2.0 * math.pi / (4 * length))
    sq = angle * angle
    sin = angle * (1.0 + sq * (F32(-1 / 6) + sq * (F32(1 / 120) + sq * (F32(-1 / 5040) + sq * F32(1 / 362880)))))
    cos = 1.0 + sq * (F32(-0.5) + sq * (F32(1 / 24) + sq * (F32(-1 / 720) + sq * (F32(1 / 40320) + sq * F32(-1 / 3628800)))))
    odd = (quad & 1) == 1
    c0 = jnp.where(odd, sin, cos)
    s0 = jnp.where(odd, cos, sin)
    c = jnp.where(((quad + 1) & 2) == 2, -c0, c0)
    s = jnp.where((quad & 2) == 2, -s0, s0)
    return c, s


def front_kernel(dims, mask_hbm, x_hbm, taps_hbm, bins_hbm, *refs):
    windows, length, factor, groups, per_group, half, rows = dims
    outs = refs[:groups]
    x_ref, mask_ref, taps_ref, bins_ref, band_ref, table_ref, lhs_ref, dec_ref, sems = refs[groups:]
    small = [
        pltpu.make_async_copy(src, dst, sems.at[n])
        for n, (src, dst) in enumerate(((taps_hbm, taps_ref), (bins_hbm, bins_ref), (mask_hbm, mask_ref)))
    ]
    for each in small:
        each.start()
    total = x_ref.shape[1]
    width = groups * 2 * half
    chunk = factor * LANES
    tiles = factor + 1
    tap_count = taps_ref.shape[1]
    chunks = -(-total // chunk)
    stages = sems.shape[0] - len(small)
    cuts = [up(chunks * k // stages, 2) for k in range(stages)] + [chunks]
    loads = []
    for k in range(stages):
        begin, end = cuts[k] * chunk, min(cuts[k + 1] * chunk, total)
        span = (0, slice(None), pl.ds(begin, end - begin))
        loads.append(pltpu.make_async_copy(x_hbm.at[span], x_ref.at[span[1:]], sems.at[len(small) + k]))
        loads[-1].start()
    for each in small:
        each.wait()

    period = math.lcm(SUB, factor)
    middle = LANES // 2
    taps = jnp.concatenate([taps_ref[...].astype(F32), jnp.zeros((1, LANES - tap_count), F32)], axis=1)
    taps = jnp.broadcast_to(taps, (SUB, LANES))
    lane8 = iota((SUB, LANES), 1)
    seeds = []
    for start in range(0, period, SUB):
        tap = factor * (lane8 - middle) + (factor - 1 + LANES - start) - iota((SUB, LANES), 0)
        tap = jnp.where((tap >= 0) & (tap < tap_count), tap, LANES - 1)
        seeds.append(jnp.take_along_axis(taps, tap, axis=1, mode="promise_in_bounds"))
    for row in range(0, tiles * LANES, 2 * SUB):
        pair = []
        for start in (row, row + SUB):
            moved = start // period * (period // factor)
            block = pltpu.roll(seeds[start % period // SUB], (moved - middle) % LANES, 1)
            if moved < 2 * SUB:
                block = jnp.where(lane8 < middle, block, 0.0)
            elif moved > LANES - 2 * SUB:
                block = jnp.where(lane8 >= middle, block, 0.0)
            pair.append(block)
        band_ref[row : row + 2 * SUB, :] = jnp.concatenate(pair, axis=0).astype(BF16)

    own = lax.axis_index("freq")
    bin_count = bins_ref.shape[1]
    held = up(bin_count, LANES)
    bins = bins_ref[...]
    if held > bin_count:
        bins = jnp.concatenate([bins, jnp.zeros((1, held - bin_count), jnp.int32)], axis=1)
    bins = jnp.broadcast_to(bins, (SUB, held))
    lane = iota((SUB, 2 * half), 1)
    is_imag = lane >= half
    valid = (lane & (half - 1)) < per_group
    blocks = up(length, 2 * LANES) // LANES
    pairs = blocks // 2
    row8 = iota((SUB, 2 * half), 0)
    table_parts = []
    for slot in range(groups):
        first = lax.rem(own + slot, groups) * per_group
        real = pltpu.roll(bins, lax.rem(held - first, held), 1)[:, : 2 * half]
        imag = pltpu.roll(bins, lax.rem(held - first + half, held), 1)[:, : 2 * half]
        bins8 = jnp.where(is_imag, imag, real)
        c, s = cos_sin(wrap((row8 + (blocks - 1) * LANES // 2) * bins8, length), length)
        near = jnp.where(valid, jnp.where(is_imag, -s, c), 0.0), jnp.where(valid, jnp.where(is_imag, -c, -s), 0.0)
        rise = [cos_sin(wrap((row8 + r) * SUB * bins8, length), length) for r in range(0, LANES // SUB, SUB)]
        apart = [cos_sin(wrap((2 * (row8 + r) + 1) * (LANES // 2) * bins8, length), length) for r in range(0, pairs, SUB)]
        table_parts.append((near, rise, apart))

    def table_rows(slot, row):
        (near_v, near_w), rise, apart = table_parts[slot]
        here = []
        for start in (row // SUB, row // SUB + 1):
            turn_c, turn_s = (t[start % SUB : start % SUB + 1] for t in rise[start // SUB])
            here.append((near_v * turn_c + near_w * turn_s, near_w * turn_c - near_v * turn_s))
        here = [jnp.concatenate(h, axis=0) for h in zip(*here)]
        for d in range(pairs):
            turn_c, turn_s = (t[d % SUB : d % SUB + 1] for t in apart[d // SUB])
            even, odd = here[0] * turn_c, here[1] * turn_s
            for block, value in ((pairs + d, even + odd), (pairs - 1 - d, even - odd)):
                table_ref[
                    block * LANES + row : block * LANES + row + 2 * SUB,
                    slot * 2 * half : (slot + 1) * 2 * half,
                ] = value.astype(BF16)

    todo = [(slot, row) for slot in range(groups) for row in range(0, LANES, 2 * SUB)]

    entries = [(q, 0) for q in range(up(chunks, 2))]
    for w in range(1, windows):
        begin = w * length * factor
        entries.append((begin // chunk, begin))
    edge = up(chunks, 2) - 1
    zero_tile = jnp.zeros((rows, LANES), F32)

    def tile_of(entry, tile):
        q, begin = entry
        start = q * chunk + (tile - 1) * LANES
        if start < 0 or start >= total or start + LANES <= begin:
            return zero_tile
        stop = min(start + LANES, total)
        got = x_ref[:, start:stop].astype(F32)
        if stop - start < LANES:
            got = jnp.concatenate([got, jnp.zeros((rows, LANES - (stop - start)), F32)], axis=1)
        if start < begin:
            got = jnp.where(lane8 >= begin - start, got, 0.0)
        return got

    if len(entries) % 2:
        entries.append((chunks + 1, 0))
    bounds = cuts[:-1] + [len(entries)]
    share = -(-len(todo) // (stages + 1))
    for slot, row in todo[:share]:
        table_rows(slot, row)
    for k in range(stages):
        loads[k].wait()
        for pair in range(bounds[k], bounds[k + 1], 2):
            for tile in range(tiles):
                both = [tile_of(entries[pair + e], tile) for e in range(2)]
                lhs_ref[pair * rows : (pair + 2) * rows, tile * LANES : (tile + 1) * LANES] = (
                    jnp.concatenate(both, axis=0).astype(BF16)
                )
        span = slice(bounds[k] * rows, bounds[k + 1] * rows)
        dec_ref[span, :] = jnp.dot(lhs_ref[span, 0 : tiles * LANES], band_ref[...], preferred_element_type=F32)
        for slot, row in todo[(k + 1) * share : (k + 2) * share]:
            table_rows(slot, row)

    def dec(entry):
        return dec_ref[entry * rows : (entry + 1) * rows, :]

    spectrum = None
    for block in range(blocks):
        parts = []
        for w in range(windows):
            first, lead = divmod(w * length, LANES)
            entry = first + block
            low = dec(edge + w) if (block == 0 and w > 0) else dec(entry)
            if lead:
                low = pltpu.roll(low, LANES - lead, 1)
                if entry + 1 < chunks:
                    high = pltpu.roll(dec(entry + 1), LANES - lead, 1)
                    low = jnp.where(lane8 < LANES - lead, low, high)
            left = length - block * LANES
            if left < LANES:
                low = jnp.where(lane8 < left, low, 0.0)
            parts.append(low)
        lhs = jnp.concatenate(parts, axis=0).astype(BF16)
        lhs_ref[0 : windows * rows, block * LANES : (block + 1) * LANES] = lhs
    spectrum = jnp.dot(
        lhs_ref[0 : windows * rows, 0 : blocks * LANES], table_ref[...], preferred_element_type=F32
    )
    power = jnp.sum(spectrum * spectrum, axis=1, keepdims=True) / bin_count
    row = iota((windows * rows, 1), 0) & (rows - 1)
    live = jnp.zeros((windows * rows, 1), F32)
    for r in range(rows):
        live = jnp.where(row == r, mask_ref[0, r].astype(F32), live)
    scale = lax.rsqrt(power + 1e-06) * live
    for slot in range(groups):
        piece = spectrum[:, slot * 2 * half : (slot + 1) * 2 * half] * scale
        outs[slot][...] = piece.astype(BF16)


def front(raw_strain, fir_taps, band_bins, live_mask, groups):
    rows = raw_strain.shape[1]
    bins = band_bins.shape[0]
    per_group = bins // groups
    half = up(per_group, 64)
    dims = (WIN, NT, DECIM, groups, per_group, half, rows)
    width = groups * 2 * half
    total = raw_strain.shape[2]
    chunks = -(-total // (DECIM * LANES))
    entries = up(up(chunks, 2) + WIN - 1, 2)
    blocks = up(NT, 2 * LANES)
    stages = 4
    vmem = pl.BlockSpec(memory_space=pltpu.VMEM)
    return pl.pallas_call(
        functools.partial(front_kernel, dims),
        out_shape=[jax.ShapeDtypeStruct((WIN * rows, 2 * half), BF16)] * groups,
        in_specs=[pl.BlockSpec(memory_space=pltpu.HBM)] * 4,
        out_specs=[vmem] * groups,
        scratch_shapes=[
            pltpu.VMEM((rows, total), BF16),
            pltpu.SMEM(live_mask.shape, jnp.int32),
            pltpu.VMEM((1, fir_taps.shape[0]), BF16),
            pltpu.VMEM((1, bins), jnp.int32),
            pltpu.VMEM(((DECIM + 1) * LANES, LANES), BF16),
            pltpu.VMEM((blocks, width), BF16),
            pltpu.VMEM((entries * rows, max((DECIM + 1) * LANES, blocks)), BF16),
            pltpu.VMEM((entries * rows, LANES), F32),
            pltpu.SemaphoreType.DMA((3 + stages,)),
        ],
        compiler_params=pltpu.CompilerParams(vmem_limit_bytes=20 << 20),
        name="front",
    )(*[
        pltpu.with_memory_space_constraint(a, pltpu.HBM)
        for a in (live_mask, raw_strain, fir_taps[None, :], band_bins[None, :])
    ])


def rows_kernel(dims, parts_ref, out_ref, turned_ref):
    windows, rows, zs, half, per_group, pack = dims
    height = rows * zs
    own = lax.axis_index("freq")
    lane = iota((height, 2 * half), 1)
    depth = 2 * windows
    blank = jnp.zeros((LANES - 2 * height, 2 * half), F32)
    for pair in range(0, windows, 2):
        mine = ([], [])
        for z in range(zs):
            slot = lax.rem(own + zs - z, zs)
            got = parts_ref[slot, pair * rows : (pair + 2) * rows, :].astype(F32)
            mine[0].append(got[:rows])
            mine[1].append(got[rows:])
        for e in range(2):
            straight = jnp.concatenate(mine[e], axis=0)
            swapped = pltpu.roll(straight, half, 1)
            swapped = jnp.where(lane < half, swapped, -swapped)
            flipped = jnp.concatenate([straight, swapped, blank], axis=0).T
            for part in range(2):
                turned_ref[pl.ds(2 * (pair + e) + part, half, stride=depth), :] = flipped[part * half : (part + 1) * half]
    lane = iota((2 * height, LANES), 1)
    for group in range(per_group // pack):
        got = turned_ref[group * pack * depth : (group + 1) * pack * depth, :]
        got = jnp.concatenate([got, jnp.zeros((LANES - pack * depth, LANES), F32)], axis=0).T[: 2 * height]
        for k in range(pack):
            inside = (lane >= k * depth) & (lane < (k + 1) * depth)
            out_ref[group, k * 2 * height : (k + 1) * 2 * height, :] = jnp.where(inside, got, 0.0).astype(BF16)


def correlate_kernel(dims, left_ref, parts_ref, out_hbm, *refs):
    windows, rows, zs, blocks, half, per_group, pack = dims
    *spec_refs, out_ref, sems = refs
    height = rows * zs
    depth = 2 * windows
    block = lax.axis_index("chan")
    own = lax.axis_index("freq")
    per_tile = LANES // height
    for pair in range(0, windows, 2):
        for tile, spec_ref in enumerate(spec_refs):
            slabs = ([], [])
            for b in range(tile * per_tile, (tile + 1) * per_tile):
                for z in range(zs):
                    slot = lax.rem(own + zs - z, zs)
                    got = parts_ref[(block ^ b) & 1, (block ^ b) >> 1, slot, pair * rows : (pair + 2) * rows, :].astype(F32)
                    slabs[0].append(got[:rows])
                    slabs[1].append(got[rows:])
            for e in range(2):
                flipped = jnp.concatenate(slabs[e], axis=0).T
                for part in range(2):
                    spec_ref[pl.ds(2 * (pair + e) + part, half, stride=depth), :] = flipped[part * half : (part + 1) * half]
    copies = []
    for group in range(per_group // pack):
        at = group * pack * depth
        right = [ref[at : at + pack * depth, :] for ref in spec_refs]
        right = jnp.concatenate(right, axis=1).astype(BF16)
        prod = jnp.dot(left_ref[group, :, : pack * depth], right, preferred_element_type=F32)
        prod = prod * F32(1.0 / windows)
        first = group * pack
        out_ref[first : first + pack] = prod.reshape(pack, 2, height, prod.shape[1])
        copies.append(pltpu.make_async_copy(out_ref.at[pl.ds(first, pack)], out_hbm.at[pl.ds(first, pack)], sems.at[group]))
        copies[-1].start()
    for each in copies:
        each.wait()


def pack_of(per_group, windows):
    return next(p for p in (4, 2, 1) if per_group % p == 0 and 2 * windows * p <= LANES)


def row_side(parts, per_group, rows):
    zs, full_rows, lanes = parts.shape
    windows = full_rows // rows
    pack = pack_of(per_group, windows)
    half = lanes // 2
    height = rows * zs
    vmem = pl.BlockSpec(memory_space=pltpu.VMEM)
    return pl.pallas_call(
        functools.partial(rows_kernel, (windows, rows, zs, half, per_group, pack)),
        out_shape=jax.ShapeDtypeStruct((per_group // pack, pack * 2 * height, LANES), BF16),
        in_specs=[vmem],
        out_specs=vmem,
        scratch_shapes=[pltpu.VMEM((half * 2 * windows, LANES), F32)],
        compiler_params=pltpu.CompilerParams(vmem_limit_bytes=8 << 20),
        cost_estimate=pl.CostEstimate(flops=1 << 24, bytes_accessed=4 << 20, transcendentals=0),
        name="rows",
    )(parts)


def correlate(left, parts, per_group, rows):
    _, chips, zs, full_rows, lanes = parts.shape
    blocks = 2 * chips
    windows = full_rows // rows
    half = lanes // 2
    height = rows * zs
    width = height * blocks
    pack = pack_of(per_group, windows)
    dims = (windows, rows, zs, blocks, half, per_group, pack)
    vmem = pl.BlockSpec(memory_space=pltpu.VMEM)
    shape = (per_group, 2, height, width)
    return pl.pallas_call(
        functools.partial(correlate_kernel, dims),
        out_shape=jax.ShapeDtypeStruct(shape, F32),
        in_specs=[vmem, vmem],
        out_specs=pl.BlockSpec(memory_space=pltpu.HBM),
        scratch_shapes=[pltpu.VMEM((half * 2 * windows, LANES), F32)] * (width // LANES)
        + [pltpu.VMEM(shape, F32), pltpu.SemaphoreType.DMA((per_group // pack,))],
        compiler_params=pltpu.CompilerParams(vmem_limit_bytes=(24 if blocks <= 8 else 44) << 20),
        name="correlate",
    )(left, parts)


def shards(groups, blocks, raw_strain, fir_taps, band_bins, live_mask):
    rows = raw_strain.shape[1]
    per_group = band_bins.shape[0] // groups
    pieces = front(raw_strain, fir_taps, band_bins, live_mask, groups)
    got = [pieces[0]]
    for slot in range(1, groups):
        pairs = [(i, (i + slot) % groups) for i in range(groups)]
        got.append(lax.ppermute(pieces[slot], "freq", pairs))
    parts = jnp.stack(got)
    left = row_side(parts, per_group, rows)
    same = [parts[None]]
    for step in range(2, blocks, 2):
        same.append(lax.ppermute(parts[None], "chan", [(i, i ^ step) for i in range(blocks)]))
    same = jnp.concatenate(same, axis=0)
    other = lax.ppermute(same, "chan", [(i, i ^ 1) for i in range(blocks)])
    both = jnp.stack([same, other])
    return correlate(left, both, per_group, rows)


def solution(mesh):
    in_specs = (P("chan", "freq", None), P(), P(), P("chan", "freq"))
    out_specs = P("freq", None, "chan", None)
    body = functools.partial(shards, mesh.shape["freq"], mesh.shape["chan"])
    return jax.shard_map(body, mesh=mesh, in_specs=in_specs, out_specs=out_specs, check_vma=False)
```

```python
import functools
import math

import jax
import jax.numpy as jnp
from jax import lax
from jax.experimental import pallas as pl
from jax.experimental.pallas import tpu as pltpu
from jax.sharding import PartitionSpec as P


WIN = 10
DECIM = 10
NT = 1500
LANES = 128
SUB = 8
F32 = jnp.float32
BF16 = jnp.bfloat16


def up(value, unit):
    return -(-value // unit) * unit


def iota(shape, axis):
    return lax.broadcasted_iota(jnp.int32, shape, axis)


def wrap(product, length):
    turns = jnp.floor((product.astype(F32) + 0.5) * F32(1.0 / length)).astype(jnp.int32)
    return product - turns * length


def cos_sin(phase, length):
    four = 4 * phase
    quad = jnp.floor((four.astype(F32) + (0.5 * length + 0.5)) * F32(1.0 / length)).astype(jnp.int32)
    angle = (four - quad * length).astype(F32) * F32(2.0 * math.pi / (4 * length))
    sq = angle * angle
    sin = angle * (1.0 + sq * (F32(-1 / 6) + sq * (F32(1 / 120) + sq * (F32(-1 / 5040) + sq * F32(1 / 362880)))))
    cos = 1.0 + sq * (F32(-0.5) + sq * (F32(1 / 24) + sq * (F32(-1 / 720) + sq * (F32(1 / 40320) + sq * F32(-1 / 3628800)))))
    odd = (quad & 1) == 1
    c0 = jnp.where(odd, sin, cos)
    s0 = jnp.where(odd, cos, sin)
    c = jnp.where(((quad + 1) & 2) == 2, -c0, c0)
    s = jnp.where((quad & 2) == 2, -s0, s0)
    return c, s


def front_kernel(dims, mask_hbm, x_hbm, taps_hbm, bins_hbm, *refs):
    windows, length, factor, groups, per_group, half, rows = dims
    outs = refs[:groups]
    x_ref, mask_ref, taps_ref, bins_ref, band_ref, table_ref, lhs_ref, dec_ref, sems = refs[groups:]
    small = [
        pltpu.make_async_copy(src, dst, sems.at[n])
        for n, (src, dst) in enumerate(((taps_hbm, taps_ref), (bins_hbm, bins_ref), (mask_hbm, mask_ref)))
    ]
    for each in small:
        each.start()
    total = x_ref.shape[1]
    chunk = factor * LANES
    tiles = factor + 1
    tap_count = taps_ref.shape[1]
    chunks = -(-total // chunk)
    stages = sems.shape[0] - len(small)
    cuts = [up(chunks * k // stages, 2) for k in range(stages)] + [chunks]
    loads = []
    for k in range(stages):
        begin, end = cuts[k] * chunk, min(cuts[k + 1] * chunk, total)
        span = (0, slice(None), pl.ds(begin, end - begin))
        loads.append(pltpu.make_async_copy(x_hbm.at[span], x_ref.at[span[1:]], sems.at[len(small) + k]))
        loads[-1].start()
    for each in small:
        each.wait()

    period = math.lcm(SUB, factor)
    middle = LANES // 2
    taps = jnp.concatenate([taps_ref[...].astype(F32), jnp.zeros((1, LANES - tap_count), F32)], axis=1)
    taps = jnp.broadcast_to(taps, (SUB, LANES))
    lane8 = iota((SUB, LANES), 1)
    seeds = []
    for start in range(0, period, SUB):
        tap = factor * (lane8 - middle) + (factor - 1 + LANES - start) - iota((SUB, LANES), 0)
        tap = jnp.where((tap >= 0) & (tap < tap_count), tap, LANES - 1)
        seeds.append(jnp.take_along_axis(taps, tap, axis=1, mode="promise_in_bounds"))
    for row in range(0, tiles * LANES, 2 * SUB):
        pair = []
        for start in (row, row + SUB):
            moved = start // period * (period // factor)
            block = pltpu.roll(seeds[start % period // SUB], (moved - middle) % LANES, 1)
            if moved < 2 * SUB:
                block = jnp.where(lane8 < middle, block, 0.0)
            elif moved > LANES - 2 * SUB:
                block = jnp.where(lane8 >= middle, block, 0.0)
            pair.append(block)
        band_ref[row : row + 2 * SUB, :] = jnp.concatenate(pair, axis=0).astype(BF16)

    own = lax.axis_index("freq")
    bin_count = bins_ref.shape[1]
    held = up(bin_count, LANES)
    bins = bins_ref[...]
    if held > bin_count:
        bins = jnp.concatenate([bins, jnp.zeros((1, held - bin_count), jnp.int32)], axis=1)
    bins = jnp.broadcast_to(bins, (SUB, held))
    lane = iota((SUB, 2 * half), 1)
    is_imag = lane >= half
    valid = (lane & (half - 1)) < per_group
    blocks = up(length, 2 * LANES) // LANES
    pairs = blocks // 2
    row8 = iota((SUB, 2 * half), 0)
    table_parts = []
    for slot in range(groups):
        first = lax.rem(own + slot, groups) * per_group
        real = pltpu.roll(bins, lax.rem(held - first, held), 1)[:, : 2 * half]
        imag = pltpu.roll(bins, lax.rem(held - first + half, held), 1)[:, : 2 * half]
        bins8 = jnp.where(is_imag, imag, real)
        c, s = cos_sin(wrap((row8 + (blocks - 1) * LANES // 2) * bins8, length), length)
        near = jnp.where(valid, jnp.where(is_imag, -s, c), 0.0), jnp.where(valid, jnp.where(is_imag, -c, -s), 0.0)
        rise = [cos_sin(wrap((row8 + r) * SUB * bins8, length), length) for r in range(0, LANES // SUB, SUB)]
        apart = [cos_sin(wrap((2 * (row8 + r) + 1) * (LANES // 2) * bins8, length), length) for r in range(0, pairs, SUB)]
        table_parts.append((near, rise, apart))

    def table_rows(slot, row):
        (near_v, near_w), rise, apart = table_parts[slot]
        here = []
        for start in (row // SUB, row // SUB + 1):
            turn_c, turn_s = (t[start % SUB : start % SUB + 1] for t in rise[start // SUB])
            here.append((near_v * turn_c + near_w * turn_s, near_w * turn_c - near_v * turn_s))
        here = [jnp.concatenate(h, axis=0) for h in zip(*here)]
        for d in range(pairs):
            turn_c, turn_s = (t[d % SUB : d % SUB + 1] for t in apart[d // SUB])
            even, odd = here[0] * turn_c, here[1] * turn_s
            for block, value in ((pairs + d, even + odd), (pairs - 1 - d, even - odd)):
                table_ref[
                    block * LANES + row : block * LANES + row + 2 * SUB,
                    slot * 2 * half : (slot + 1) * 2 * half,
                ] = value.astype(BF16)

    todo = [(slot, row) for slot in range(groups) for row in range(0, LANES, 2 * SUB)]

    entries = [(q, 0) for q in range(up(chunks, 2))]
    for w in range(1, windows):
        begin = w * length * factor
        entries.append((begin // chunk, begin))
    edge = up(chunks, 2) - 1
    zero_tile = jnp.zeros((rows, LANES), F32)

    def tile_of(entry, tile):
        q, begin = entry
        start = q * chunk + (tile - 1) * LANES
        if start < 0 or start >= total or start + LANES <= begin:
            return zero_tile
        stop = min(start + LANES, total)
        got = x_ref[:, start:stop].astype(F32)
        if stop - start < LANES:
            got = jnp.concatenate([got, jnp.zeros((rows, LANES - (stop - start)), F32)], axis=1)
        if start < begin:
            got = jnp.where(lane8 >= begin - start, got, 0.0)
        return got

    if len(entries) % 2:
        entries.append((chunks + 1, 0))
    bounds = cuts[:-1] + [len(entries)]
    share = -(-len(todo) // (stages + 1))
    for slot, row in todo[:share]:
        table_rows(slot, row)
    for k in range(stages):
        loads[k].wait()
        for pair in range(bounds[k], bounds[k + 1], 2):
            for tile in range(tiles):
                both = [tile_of(entries[pair + e], tile) for e in range(2)]
                lhs_ref[pair * rows : (pair + 2) * rows, tile * LANES : (tile + 1) * LANES] = (
                    jnp.concatenate(both, axis=0).astype(BF16)
                )
        span = slice(bounds[k] * rows, bounds[k + 1] * rows)
        dec_ref[span, :] = jnp.dot(lhs_ref[span, 0 : tiles * LANES], band_ref[...], preferred_element_type=F32)
        for slot, row in todo[(k + 1) * share : (k + 2) * share]:
            table_rows(slot, row)

    def dec(entry):
        return dec_ref[entry * rows : (entry + 1) * rows, :]

    spectrum = None
    for block in range(blocks):
        parts = []
        for w in range(windows):
            first, lead = divmod(w * length, LANES)
            entry = first + block
            low = dec(edge + w) if (block == 0 and w > 0) else dec(entry)
            if lead:
                low = pltpu.roll(low, LANES - lead, 1)
                if entry + 1 < chunks:
                    high = pltpu.roll(dec(entry + 1), LANES - lead, 1)
                    low = jnp.where(lane8 < LANES - lead, low, high)
            left = length - block * LANES
            if left < LANES:
                low = jnp.where(lane8 < left, low, 0.0)
            parts.append(low)
        lhs = jnp.concatenate(parts, axis=0).astype(BF16)
        lhs_ref[0 : windows * rows, block * LANES : (block + 1) * LANES] = lhs
    spectrum = jnp.dot(
        lhs_ref[0 : windows * rows, 0 : blocks * LANES], table_ref[...], preferred_element_type=F32
    )
    power = jnp.sum(spectrum * spectrum, axis=1, keepdims=True) / bin_count
    row = iota((windows * rows, 1), 0) & (rows - 1)
    live = jnp.zeros((windows * rows, 1), F32)
    for r in range(rows):
        live = jnp.where(row == r, mask_ref[0, r].astype(F32), live)
    scale = lax.rsqrt(power + 1e-06) * live
    for slot in range(groups):
        piece = spectrum[:, slot * 2 * half : (slot + 1) * 2 * half] * scale
        outs[slot][...] = piece.astype(BF16)


def front(raw_strain, fir_taps, band_bins, live_mask, groups):
    rows = raw_strain.shape[1]
    bins = band_bins.shape[0]
    per_group = bins // groups
    half = up(per_group, 64)
    dims = (WIN, NT, DECIM, groups, per_group, half, rows)
    width = groups * 2 * half
    total = raw_strain.shape[2]
    chunks = -(-total // (DECIM * LANES))
    entries = up(up(chunks, 2) + WIN - 1, 2)
    blocks = up(NT, 2 * LANES)
    stages = 4
    vmem = pl.BlockSpec(memory_space=pltpu.VMEM)
    return pl.pallas_call(
        functools.partial(front_kernel, dims),
        out_shape=[jax.ShapeDtypeStruct((WIN * rows, 2 * half), BF16)] * groups,
        in_specs=[pl.BlockSpec(memory_space=pltpu.HBM)] * 4,
        out_specs=[vmem] * groups,
        scratch_shapes=[
            pltpu.VMEM((rows, total), BF16),
            pltpu.SMEM(live_mask.shape, jnp.int32),
            pltpu.VMEM((1, fir_taps.shape[0]), BF16),
            pltpu.VMEM((1, bins), jnp.int32),
            pltpu.VMEM(((DECIM + 1) * LANES, LANES), BF16),
            pltpu.VMEM((blocks, width), BF16),
            pltpu.VMEM((entries * rows, max((DECIM + 1) * LANES, blocks)), BF16),
            pltpu.VMEM((entries * rows, LANES), F32),
            pltpu.SemaphoreType.DMA((3 + stages,)),
        ],
        compiler_params=pltpu.CompilerParams(vmem_limit_bytes=20 << 20),
        name="front",
    )(*[
        pltpu.with_memory_space_constraint(a, pltpu.HBM)
        for a in (live_mask, raw_strain, fir_taps[None, :], band_bins[None, :])
    ])


def rows_kernel(dims, parts_ref, out_ref, turned_ref):
    windows, rows, zs, half, per_group, pack = dims
    height = rows * zs
    own = lax.axis_index("freq")
    lane = iota((height, 2 * half), 1)
    depth = 2 * windows
    blank = jnp.zeros((LANES - 2 * height, 2 * half), F32)
    for pair in range(0, windows, 2):
        mine = ([], [])
        for z in range(zs):
            slot = lax.rem(own + zs - z, zs)
            got = parts_ref[slot, pair * rows : (pair + 2) * rows, :].astype(F32)
            mine[0].append(got[:rows])
            mine[1].append(got[rows:])
        for e in range(2):
            straight = jnp.concatenate(mine[e], axis=0)
            swapped = pltpu.roll(straight, half, 1)
            swapped = jnp.where(lane < half, swapped, -swapped)
            flipped = jnp.concatenate([straight, swapped, blank], axis=0).T
            for part in range(2):
                turned_ref[pl.ds(2 * (pair + e) + part, half, stride=depth), :] = flipped[part * half : (part + 1) * half]
    lane = iota((2 * height, LANES), 1)
    for group in range(per_group // pack):
        got = turned_ref[group * pack * depth : (group + 1) * pack * depth, :]
        got = jnp.concatenate([got, jnp.zeros((LANES - pack * depth, LANES), F32)], axis=0).T[: 2 * height]
        for k in range(pack):
            inside = (lane >= k * depth) & (lane < (k + 1) * depth)
            out_ref[group, k * 2 * height : (k + 1) * 2 * height, :] = jnp.where(inside, got, 0.0).astype(BF16)


def correlate_kernel(dims, first_tile, left_ref, parts_ref, *refs):
    windows, rows, zs, half, per_group, pack, tiles = dims
    out_hbm, *spec_refs, out_ref, sems = refs if first_tile == 0 else refs[1:]
    height = rows * zs
    depth = 2 * windows
    per_tile = LANES // height
    block = lax.axis_index("chan")
    own = lax.axis_index("freq")
    own_tile, place = block // per_tile, lax.rem(block, per_tile)
    for pair in range(0, windows, 2):
        for tile, spec_ref in enumerate(spec_refs):
            slabs = ([], [])
            for b in range(per_tile):
                far = place ^ b
                for z in range(zs):
                    slot = lax.rem(own + zs - z, zs)
                    at = (far & 1, tile * (per_tile // 2) + (far >> 1), slot, slice(pair * rows, (pair + 2) * rows))
                    got = parts_ref[at].astype(F32)
                    slabs[0].append(got[:rows])
                    slabs[1].append(got[rows:])
            for e in range(2):
                flipped = jnp.concatenate(slabs[e], axis=0).T
                for part in range(2):
                    spec_ref[pl.ds(2 * (pair + e) + part, half, stride=depth), :] = flipped[part * half : (part + 1) * half]
    copies = []
    for group in range(per_group // pack):
        at = group * pack * depth
        right = [ref[at : at + pack * depth, :] for ref in spec_refs]
        right = jnp.concatenate(right, axis=1).astype(BF16)
        prod = jnp.dot(left_ref[group, :, : pack * depth], right, preferred_element_type=F32)
        prod = prod * F32(1.0 / windows)
        first = group * pack
        for tile in range(tiles):
            out_ref[tile, first : first + pack] = prod[:, tile * LANES : (tile + 1) * LANES].reshape(pack, 2, height, LANES)
            columns = pl.ds(pl.multiple_of((own_tile ^ (first_tile + tile)) * LANES, LANES), LANES)
            copies.append(pltpu.make_async_copy(
                out_ref.at[tile, pl.ds(first, pack)],
                out_hbm.at[pl.ds(first, pack), :, :, columns],
                sems.at[group, tile],
            ))
            copies[-1].start()
    for each in copies:
        each.wait()


def pack_of(per_group, windows):
    return next(p for p in (4, 2, 1) if per_group % p == 0 and 2 * windows * p <= LANES)


def row_side(parts, per_group, rows):
    zs, full_rows, lanes = parts.shape
    windows = full_rows // rows
    pack = pack_of(per_group, windows)
    half = lanes // 2
    height = rows * zs
    vmem = pl.BlockSpec(memory_space=pltpu.VMEM)
    return pl.pallas_call(
        functools.partial(rows_kernel, (windows, rows, zs, half, per_group, pack)),
        out_shape=jax.ShapeDtypeStruct((per_group // pack, pack * 2 * height, LANES), BF16),
        in_specs=[vmem],
        out_specs=vmem,
        scratch_shapes=[pltpu.VMEM((half * 2 * windows, LANES), F32)],
        compiler_params=pltpu.CompilerParams(vmem_limit_bytes=8 << 20),
        cost_estimate=pl.CostEstimate(flops=1 << 24, bytes_accessed=4 << 20, transcendentals=0),
        name="rows",
    )(parts)


def correlate(left, parts, width, first_tile, per_group, rows, so_far=None):
    _, chips, zs, full_rows, lanes = parts.shape
    windows = full_rows // rows
    half = lanes // 2
    height = rows * zs
    tiles = chips * 2 * height // LANES
    pack = pack_of(per_group, windows)
    dims = (windows, rows, zs, half, per_group, pack, tiles)
    vmem = pl.BlockSpec(memory_space=pltpu.VMEM)
    hbm = pl.BlockSpec(memory_space=pltpu.HBM)
    given = [] if so_far is None else [so_far]
    written = per_group * 2 * height * tiles * LANES
    return pl.pallas_call(
        functools.partial(correlate_kernel, dims, first_tile),
        out_shape=jax.ShapeDtypeStruct((per_group, 2, height, width), F32),
        in_specs=[vmem, vmem] + [hbm] * len(given),
        out_specs=hbm,
        input_output_aliases={2: 0} if given else {},
        scratch_shapes=[pltpu.VMEM((half * 2 * windows, LANES), F32)] * tiles
        + [pltpu.VMEM((tiles, per_group, 2, height, LANES), F32), pltpu.SemaphoreType.DMA((per_group // pack, tiles))],
        compiler_params=pltpu.CompilerParams(vmem_limit_bytes=(12 if tiles <= 2 else 44) << 20),
        cost_estimate=pl.CostEstimate(flops=written * 4 * windows, bytes_accessed=written * 4, transcendentals=0),
        name="correlate",
    )(left, parts, *given)


def shards(groups, blocks, raw_strain, fir_taps, band_bins, live_mask):
    rows = raw_strain.shape[1]
    per_group = band_bins.shape[0] // groups
    pieces = front(raw_strain, fir_taps, band_bins, live_mask, groups)
    got = [pieces[0]]
    for slot in range(1, groups):
        pairs = [(i, (i + slot) % groups) for i in range(groups)]
        got.append(lax.ppermute(pieces[slot], "freq", pairs))
    parts = jnp.stack(got)[None]
    left = row_side(parts[0], per_group, rows)

    def swap(array, step):
        return lax.ppermute(array, "chan", [(i, i ^ step) for i in range(blocks)])

    shared = LANES // (rows * groups) // 2
    chips = [parts] + [swap(parts, step) for step in range(2, blocks, 2)]
    near = jnp.concatenate(chips[:shared], axis=0)
    near, left = lax.optimization_barrier((near, left))
    near = jnp.stack([near, swap(near, 1)])
    width = blocks * rows * groups
    far = jnp.concatenate(chips[shared:], axis=0) if len(chips) > shared else None
    if far is not None:
        far, near = lax.optimization_barrier((far, near))
        far = jnp.stack([far, swap(far, 1)])
    out = correlate(left, near, width, 0, per_group, rows)
    if far is not None:
        out = correlate(left, far, width, 1, per_group, rows, out)
    return out


def solution(mesh):
    in_specs = (P("chan", "freq", None), P(), P(), P("chan", "freq"))
    out_specs = P("freq", None, "chan", None)
    blocks = mesh.shape["chan"]
    body = functools.partial(shards, mesh.shape["freq"], blocks)

    return jax.shard_map(body, mesh=mesh, in_specs=in_specs, out_specs=out_specs, check_vma=False)
```

```python
import functools
import math

import jax
import jax.numpy as jnp
from jax import lax
from jax.experimental import pallas as pl
from jax.experimental.pallas import tpu as pltpu
from jax.sharding import PartitionSpec as P


WIN = 10
DECIM = 10
NT = 1500
LANES = 128
SUB = 8
F32 = jnp.float32
BF16 = jnp.bfloat16


def up(value, unit):
    return -(-value // unit) * unit


def iota(shape, axis):
    return lax.broadcasted_iota(jnp.int32, shape, axis)


def wrap(product, length):
    turns = jnp.floor((product.astype(F32) + 0.5) * F32(1.0 / length)).astype(jnp.int32)
    return product - turns * length


def cos_sin(phase, length):
    four = 4 * phase
    quad = jnp.floor((four.astype(F32) + (0.5 * length + 0.5)) * F32(1.0 / length)).astype(jnp.int32)
    angle = (four - quad * length).astype(F32) * F32(2.0 * math.pi / (4 * length))
    sq = angle * angle
    sin = angle * (1.0 + sq * (F32(-1 / 6) + sq * (F32(1 / 120) + sq * (F32(-1 / 5040) + sq * F32(1 / 362880)))))
    cos = 1.0 + sq * (F32(-0.5) + sq * (F32(1 / 24) + sq * (F32(-1 / 720) + sq * (F32(1 / 40320) + sq * F32(-1 / 3628800)))))
    odd = (quad & 1) == 1
    c0 = jnp.where(odd, sin, cos)
    s0 = jnp.where(odd, cos, sin)
    c = jnp.where(((quad + 1) & 2) == 2, -c0, c0)
    s = jnp.where((quad & 2) == 2, -s0, s0)
    return c, s


def front_kernel(dims, mask_hbm, x_hbm, taps_hbm, bins_hbm, *refs):
    windows, length, factor, groups, per_group, half, rows = dims
    outs = refs[:groups]
    x_ref, mask_ref, taps_ref, bins_ref, band_ref, table_ref, lhs_ref, dec_ref, sems = refs[groups:]
    small = [
        pltpu.make_async_copy(src, dst, sems.at[n])
        for n, (src, dst) in enumerate(((taps_hbm, taps_ref), (bins_hbm, bins_ref), (mask_hbm, mask_ref)))
    ]
    for each in small:
        each.start()
    total = x_ref.shape[1]
    chunk = factor * LANES
    tiles = factor + 1
    tap_count = taps_ref.shape[1]
    chunks = -(-total // chunk)
    stages = sems.shape[0] - len(small)
    cuts = [up(chunks * k // stages, 2) for k in range(stages)] + [chunks]
    loads = []
    for k in range(stages):
        begin, end = cuts[k] * chunk, min(cuts[k + 1] * chunk, total)
        span = (0, slice(None), pl.ds(begin, end - begin))
        loads.append(pltpu.make_async_copy(x_hbm.at[span], x_ref.at[span[1:]], sems.at[len(small) + k]))
        loads[-1].start()
    for each in small:
        each.wait()

    period = math.lcm(SUB, factor)
    middle = LANES // 2
    taps = jnp.concatenate([taps_ref[...].astype(F32), jnp.zeros((1, LANES - tap_count), F32)], axis=1)
    taps = jnp.broadcast_to(taps, (SUB, LANES))
    lane8 = iota((SUB, LANES), 1)
    seeds = []
    for start in range(0, period, SUB):
        tap = factor * (lane8 - middle) + (factor - 1 + LANES - start) - iota((SUB, LANES), 0)
        tap = jnp.where((tap >= 0) & (tap < tap_count), tap, LANES - 1)
        seeds.append(jnp.take_along_axis(taps, tap, axis=1, mode="promise_in_bounds"))
    for row in range(0, tiles * LANES, 2 * SUB):
        pair = []
        for start in (row, row + SUB):
            moved = start // period * (period // factor)
            block = pltpu.roll(seeds[start % period // SUB], (moved - middle) % LANES, 1)
            if moved < 2 * SUB:
                block = jnp.where(lane8 < middle, block, 0.0)
            elif moved > LANES - 2 * SUB:
                block = jnp.where(lane8 >= middle, block, 0.0)
            pair.append(block)
        band_ref[row : row + 2 * SUB, :] = jnp.concatenate(pair, axis=0).astype(BF16)

    own = lax.axis_index("freq")
    bin_count = bins_ref.shape[1]
    held = up(bin_count, LANES)
    bins = bins_ref[...]
    if held > bin_count:
        bins = jnp.concatenate([bins, jnp.zeros((1, held - bin_count), jnp.int32)], axis=1)
    bins = jnp.broadcast_to(bins, (SUB, held))
    lane = iota((SUB, 2 * half), 1)
    is_imag = lane >= half
    valid = (lane & (half - 1)) < per_group
    blocks = up(length, 2 * LANES) // LANES
    pairs = blocks // 2
    row8 = iota((SUB, 2 * half), 0)
    table_parts = []
    for slot in range(groups):
        first = lax.rem(own + slot, groups) * per_group
        real = pltpu.roll(bins, lax.rem(held - first, held), 1)[:, : 2 * half]
        imag = pltpu.roll(bins, lax.rem(held - first + half, held), 1)[:, : 2 * half]
        bins8 = jnp.where(is_imag, imag, real)
        c, s = cos_sin(wrap((row8 + (blocks - 1) * LANES // 2) * bins8, length), length)
        near = jnp.where(valid, jnp.where(is_imag, -s, c), 0.0), jnp.where(valid, jnp.where(is_imag, -c, -s), 0.0)
        rise = [cos_sin(wrap((row8 + r) * SUB * bins8, length), length) for r in range(0, LANES // SUB, SUB)]
        apart = [cos_sin(wrap((2 * (row8 + r) + 1) * (LANES // 2) * bins8, length), length) for r in range(0, pairs, SUB)]
        table_parts.append((near, rise, apart))

    def table_rows(slot, row):
        (near_v, near_w), rise, apart = table_parts[slot]
        here = []
        for start in (row // SUB, row // SUB + 1):
            turn_c, turn_s = (t[start % SUB : start % SUB + 1] for t in rise[start // SUB])
            here.append((near_v * turn_c + near_w * turn_s, near_w * turn_c - near_v * turn_s))
        here = [jnp.concatenate(h, axis=0) for h in zip(*here)]
        for d in range(pairs):
            turn_c, turn_s = (t[d % SUB : d % SUB + 1] for t in apart[d // SUB])
            even, odd = here[0] * turn_c, here[1] * turn_s
            for block, value in ((pairs + d, even + odd), (pairs - 1 - d, even - odd)):
                table_ref[
                    block * LANES + row : block * LANES + row + 2 * SUB,
                    slot * 2 * half : (slot + 1) * 2 * half,
                ] = value.astype(BF16)

    todo = [(slot, row) for slot in range(groups) for row in range(0, LANES, 2 * SUB)]

    entries = [(q, 0) for q in range(up(chunks, 2))]
    for w in range(1, windows):
        begin = w * length * factor
        entries.append((begin // chunk, begin))
    edge = up(chunks, 2) - 1
    zero_tile = jnp.zeros((rows, LANES), F32)

    def tile_of(entry, tile):
        q, begin = entry
        start = q * chunk + (tile - 1) * LANES
        if start < 0 or start >= total or start + LANES <= begin:
            return zero_tile
        stop = min(start + LANES, total)
        got = x_ref[:, start:stop].astype(F32)
        if stop - start < LANES:
            got = jnp.concatenate([got, jnp.zeros((rows, LANES - (stop - start)), F32)], axis=1)
        if start < begin:
            got = jnp.where(lane8 >= begin - start, got, 0.0)
        return got

    if len(entries) % 2:
        entries.append((chunks + 1, 0))
    bounds = cuts[:-1] + [len(entries)]
    share = -(-len(todo) // (stages + 1))
    for slot, row in todo[:share]:
        table_rows(slot, row)
    for k in range(stages):
        loads[k].wait()
        for pair in range(bounds[k], bounds[k + 1], 2):
            for tile in range(tiles):
                both = [tile_of(entries[pair + e], tile) for e in range(2)]
                lhs_ref[pair * rows : (pair + 2) * rows, tile * LANES : (tile + 1) * LANES] = (
                    jnp.concatenate(both, axis=0).astype(BF16)
                )
        span = slice(bounds[k] * rows, bounds[k + 1] * rows)
        dec_ref[span, :] = jnp.dot(lhs_ref[span, 0 : tiles * LANES], band_ref[...], preferred_element_type=F32)
        for slot, row in todo[(k + 1) * share : (k + 2) * share]:
            table_rows(slot, row)

    def dec(entry):
        return dec_ref[entry * rows : (entry + 1) * rows, :]

    spectrum = None
    for block in range(blocks):
        parts = []
        for w in range(windows):
            first, lead = divmod(w * length, LANES)
            entry = first + block
            low = dec(edge + w) if (block == 0 and w > 0) else dec(entry)
            if lead:
                low = pltpu.roll(low, LANES - lead, 1)
                if entry + 1 < chunks:
                    high = pltpu.roll(dec(entry + 1), LANES - lead, 1)
                    low = jnp.where(lane8 < LANES - lead, low, high)
            left = length - block * LANES
            if left < LANES:
                low = jnp.where(lane8 < left, low, 0.0)
            parts.append(low)
        lhs = jnp.concatenate(parts, axis=0).astype(BF16)
        lhs_ref[0 : windows * rows, block * LANES : (block + 1) * LANES] = lhs
    spectrum = jnp.dot(
        lhs_ref[0 : windows * rows, 0 : blocks * LANES], table_ref[...], preferred_element_type=F32
    )
    power = jnp.sum(spectrum * spectrum, axis=1, keepdims=True) / bin_count
    row = iota((windows * rows, 1), 0) & (rows - 1)
    live = jnp.zeros((windows * rows, 1), F32)
    for r in range(rows):
        live = jnp.where(row == r, mask_ref[0, r].astype(F32), live)
    scale = lax.rsqrt(power + 1e-06) * live
    for slot in range(groups):
        piece = spectrum[:, slot * 2 * half : (slot + 1) * 2 * half] * scale
        outs[slot][...] = piece.astype(BF16)


def front(raw_strain, fir_taps, band_bins, live_mask, groups):
    rows = raw_strain.shape[1]
    bins = band_bins.shape[0]
    per_group = bins // groups
    half = up(per_group, 64)
    dims = (WIN, NT, DECIM, groups, per_group, half, rows)
    width = groups * 2 * half
    total = raw_strain.shape[2]
    chunks = -(-total // (DECIM * LANES))
    entries = up(up(chunks, 2) + WIN - 1, 2)
    blocks = up(NT, 2 * LANES)
    stages = 4
    vmem = pl.BlockSpec(memory_space=pltpu.VMEM)
    return pl.pallas_call(
        functools.partial(front_kernel, dims),
        out_shape=[jax.ShapeDtypeStruct((WIN * rows, 2 * half), BF16)] * groups,
        in_specs=[pl.BlockSpec(memory_space=pltpu.HBM)] * 4,
        out_specs=[vmem] * groups,
        scratch_shapes=[
            pltpu.VMEM((rows, total), BF16),
            pltpu.SMEM(live_mask.shape, jnp.int32),
            pltpu.VMEM((1, fir_taps.shape[0]), BF16),
            pltpu.VMEM((1, bins), jnp.int32),
            pltpu.VMEM(((DECIM + 1) * LANES, LANES), BF16),
            pltpu.VMEM((blocks, width), BF16),
            pltpu.VMEM((entries * rows, max((DECIM + 1) * LANES, blocks)), BF16),
            pltpu.VMEM((entries * rows, LANES), F32),
            pltpu.SemaphoreType.DMA((3 + stages,)),
        ],
        compiler_params=pltpu.CompilerParams(vmem_limit_bytes=20 << 20),
        name="front",
    )(*[
        pltpu.with_memory_space_constraint(a, pltpu.HBM)
        for a in (live_mask, raw_strain, fir_taps[None, :], band_bins[None, :])
    ])


def rows_kernel(dims, parts_ref, out_ref, turned_ref):
    windows, rows, zs, half, per_group, pack = dims
    height = rows * zs
    own = lax.axis_index("freq")
    lane = iota((height, 2 * half), 1)
    depth = 2 * windows
    blank = jnp.zeros((LANES - 2 * height, 2 * half), F32)
    for pair in range(0, windows, 2):
        mine = ([], [])
        for z in range(zs):
            slot = lax.rem(own + zs - z, zs)
            got = parts_ref[slot, pair * rows : (pair + 2) * rows, :].astype(F32)
            mine[0].append(got[:rows])
            mine[1].append(got[rows:])
        for e in range(2):
            straight = jnp.concatenate(mine[e], axis=0)
            swapped = pltpu.roll(straight, half, 1)
            swapped = jnp.where(lane < half, swapped, -swapped)
            flipped = jnp.concatenate([straight, swapped, blank], axis=0).T
            for part in range(2):
                turned_ref[pl.ds(2 * (pair + e) + part, half, stride=depth), :] = flipped[part * half : (part + 1) * half]
    both = 2 * pack * depth
    for first in range(0, per_group // pack, 2):
        at = first * pack * depth
        size = min(both, turned_ref.shape[0] - at)
        got = turned_ref[at : at + size, :]
        got = jnp.concatenate([got, jnp.zeros((LANES - size, LANES), F32)], axis=0).T[: 2 * height]
        out_ref[first] = got.astype(BF16)
        if first + 1 < per_group // pack:
            out_ref[first + 1] = pltpu.roll(got, LANES - pack * depth, 1).astype(BF16)


def correlate_kernel(dims, first_tile, left_ref, parts_ref, *refs):
    windows, rows, zs, half, per_group, pack, tiles = dims
    out_hbm, *spec_refs, out_ref, sems = refs if first_tile == 0 else refs[1:]
    height = rows * zs
    depth = 2 * windows
    per_tile = LANES // height
    block = lax.axis_index("chan")
    own = lax.axis_index("freq")
    own_tile, place = block // per_tile, lax.rem(block, per_tile)
    for pair in range(0, windows, 2):
        for tile, spec_ref in enumerate(spec_refs):
            slabs = ([], [])
            for b in range(per_tile):
                far = place ^ b
                for z in range(zs):
                    slot = lax.rem(own + zs - z, zs)
                    at = (far & 1, tile * (per_tile // 2) + (far >> 1), slot, slice(pair * rows, (pair + 2) * rows))
                    got = parts_ref[at].astype(F32)
                    slabs[0].append(got[:rows])
                    slabs[1].append(got[rows:])
            for e in range(2):
                flipped = jnp.concatenate(slabs[e], axis=0).T
                for part in range(2):
                    spec_ref[pl.ds(2 * (pair + e) + part, half, stride=depth), :] = flipped[part * half : (part + 1) * half]
    copies = []
    row = iota((pack * depth, LANES), 0)
    burst = 2 if per_group // pack % 2 == 0 else 1
    for group in range(per_group // pack):
        at = group * pack * depth
        for tile in range(tiles):
            got = spec_refs[tile][at : at + pack * depth, :]
            right = [jnp.where((row >= k * depth) & (row < (k + 1) * depth), got, 0.0) for k in range(pack)]
            right = jnp.concatenate(right, axis=1).astype(BF16)
            prod = jnp.dot(left_ref[group, :, : pack * depth], right, preferred_element_type=F32)
            prod = prod * F32(1.0 / windows)
            for k in range(pack):
                out_ref[tile, group * pack + k] = prod[:, k * LANES : (k + 1) * LANES].reshape(2, height, LANES)
            if group % burst == burst - 1:
                span = pl.ds((group - burst + 1) * pack, burst * pack)
                columns = pl.ds(pl.multiple_of((own_tile ^ (first_tile + tile)) * LANES, LANES), LANES)
                copies.append(pltpu.make_async_copy(
                    out_ref.at[tile, span], out_hbm.at[span, :, :, columns], sems.at[group, tile]
                ))
                copies[-1].start()
    for each in copies:
        each.wait()


def pack_of(per_group, windows):
    return next(p for p in (2, 1) if per_group % p == 0 and 4 * windows * p <= LANES)


def row_side(parts, per_group, rows):
    zs, full_rows, lanes = parts.shape
    windows = full_rows // rows
    pack = pack_of(per_group, windows)
    half = lanes // 2
    height = rows * zs
    vmem = pl.BlockSpec(memory_space=pltpu.VMEM)
    return pl.pallas_call(
        functools.partial(rows_kernel, (windows, rows, zs, half, per_group, pack)),
        out_shape=jax.ShapeDtypeStruct((per_group // pack, 2 * height, LANES), BF16),
        in_specs=[vmem],
        out_specs=vmem,
        scratch_shapes=[pltpu.VMEM((half * 2 * windows, LANES), F32)],
        compiler_params=pltpu.CompilerParams(vmem_limit_bytes=8 << 20),
        cost_estimate=pl.CostEstimate(flops=1 << 24, bytes_accessed=4 << 20, transcendentals=0),
        name="rows",
    )(parts)


def correlate(left, parts, width, first_tile, per_group, rows, so_far=None):
    _, chips, zs, full_rows, lanes = parts.shape
    windows = full_rows // rows
    half = lanes // 2
    height = rows * zs
    tiles = chips * 2 * height // LANES
    pack = pack_of(per_group, windows)
    dims = (windows, rows, zs, half, per_group, pack, tiles)
    vmem = pl.BlockSpec(memory_space=pltpu.VMEM)
    hbm = pl.BlockSpec(memory_space=pltpu.HBM)
    given = [] if so_far is None else [so_far]
    written = per_group * 2 * height * tiles * LANES
    return pl.pallas_call(
        functools.partial(correlate_kernel, dims, first_tile),
        out_shape=jax.ShapeDtypeStruct((per_group, 2, height, width), F32),
        in_specs=[vmem, vmem] + [hbm] * len(given),
        out_specs=hbm,
        input_output_aliases={2: 0} if given else {},
        scratch_shapes=[pltpu.VMEM((half * 2 * windows, LANES), F32)] * tiles
        + [pltpu.VMEM((tiles, per_group, 2, height, LANES), F32), pltpu.SemaphoreType.DMA((per_group // pack, tiles))],
        compiler_params=pltpu.CompilerParams(vmem_limit_bytes=(12 if tiles <= 2 else 44) << 20),
        cost_estimate=pl.CostEstimate(flops=written * 4 * windows, bytes_accessed=written * 4, transcendentals=0),
        name="correlate",
    )(left, parts, *given)


def shards(groups, blocks, raw_strain, fir_taps, band_bins, live_mask):
    rows = raw_strain.shape[1]
    per_group = band_bins.shape[0] // groups
    pieces = front(raw_strain, fir_taps, band_bins, live_mask, groups)
    got = [pieces[0]]
    for slot in range(1, groups):
        pairs = [(i, (i + slot) % groups) for i in range(groups)]
        got.append(lax.ppermute(pieces[slot], "freq", pairs))
    parts = jnp.stack(got)[None]
    left = row_side(parts[0], per_group, rows)

    def swap(array, step):
        return lax.ppermute(array, "chan", [(i, i ^ step) for i in range(blocks)])

    shared = LANES // (rows * groups) // 2
    chips = [parts] + [swap(parts, step) for step in range(2, blocks, 2)]
    near = jnp.concatenate(chips[:shared], axis=0)
    near, left = lax.optimization_barrier((near, left))
    near = jnp.stack([near, swap(near, 1)])
    width = blocks * rows * groups
    far = jnp.concatenate(chips[shared:], axis=0) if len(chips) > shared else None
    if far is not None:
        far, near = lax.optimization_barrier((far, near))
        far = jnp.stack([far, swap(far, 1)])
    out = correlate(left, near, width, 0, per_group, rows)
    if far is not None:
        out = correlate(left, far, width, 1, per_group, rows, out)
    return out


def solution(mesh):
    in_specs = (P("chan", "freq", None), P(), P(), P("chan", "freq"))
    out_specs = P("freq", None, "chan", None)
    blocks = mesh.shape["chan"]
    body = functools.partial(shards, mesh.shape["freq"], blocks)

    return jax.shard_map(body, mesh=mesh, in_specs=in_specs, out_specs=out_specs, check_vma=False)
```

```python
import functools
import math

import jax
import jax.numpy as jnp
from jax import lax
from jax.experimental import pallas as pl
from jax.experimental.pallas import tpu as pltpu
from jax.sharding import PartitionSpec as P

WIN = 10
DECIM = 10
NT = 1500
LANES = 128
SUB = 8
F32 = jnp.float32
BF16 = jnp.bfloat16


def up(value, unit):
    return -(-value // unit) * unit


def iota(shape, axis):
    return lax.broadcasted_iota(jnp.int32, shape, axis)


def wrap(product, length):
    turns = jnp.floor((product.astype(F32) + 0.5) * F32(1.0 / length)).astype(jnp.int32)
    return product - turns * length


def cos_sin(phase, length):
    four = 4 * phase
    quad = jnp.floor((four.astype(F32) + (0.5 * length + 0.5)) * F32(1.0 / length)).astype(jnp.int32)
    angle = (four - quad * length).astype(F32) * F32(2.0 * math.pi / (4 * length))
    sq = angle * angle
    sin = angle * (1.0 + sq * (F32(-1 / 6) + sq * (F32(1 / 120) + sq * (F32(-1 / 5040) + sq * F32(1 / 362880)))))
    cos = 1.0 + sq * (F32(-0.5) + sq * (F32(1 / 24) + sq * (F32(-1 / 720) + sq * (F32(1 / 40320) + sq * F32(-1 / 3628800)))))
    odd = (quad & 1) == 1
    c0 = jnp.where(odd, sin, cos)
    s0 = jnp.where(odd, cos, sin)
    c = jnp.where(((quad + 1) & 2) == 2, -c0, c0)
    s = jnp.where((quad & 2) == 2, -s0, s0)
    return c, s


def stage_cuts(chunks, stages):
    parts = [5, 5, 4, 2][-stages:]
    return [up(chunks * sum(parts[:k]) // sum(parts), 2) for k in range(stages)] + [chunks]


def front_kernel(dims, mask_hbm, x_hbm, taps_hbm, bins_hbm, *refs):
    windows, length, factor, groups, per_group, half, rows = dims
    outs = refs[:groups]
    tail_ref, mask_ref, taps_ref, bins_ref, band_ref, table_ref, lhs_ref, dec_ref, carry_ref, rows_ref, sems = refs[groups:]
    small = [
        pltpu.make_async_copy(src, dst, sems.at[n])
        for n, (src, dst) in enumerate(((taps_hbm, taps_ref), (bins_hbm, bins_ref), (mask_hbm, mask_ref)))
    ]
    for each in small:
        each.start()
    total = x_hbm.shape[2]
    width = groups * 2 * half
    chunk = factor * LANES
    tap_count = taps_ref.shape[1]
    whole = total // chunk
    chunks = -(-total // chunk)
    stages = sems.shape[0] - len(small) - 1
    cuts = stage_cuts(chunks, stages)

    bounds, copied, chunk_at, first_at = [0], [], {}, {}
    for k in range(stages):
        at = bounds[-1]
        chunk_at.update((q, at + q - cuts[k]) for q in range(cuts[k], cuts[k + 1]))
        copied.append(slice(at * rows, (at + min(cuts[k + 1], whole) - cuts[k]) * rows))
        at += cuts[k + 1] - cuts[k]
        for w in range(1, windows):
            if cuts[k] <= w * length * factor // chunk < cuts[k + 1]:
                first_at[w] = at
                at += 1
        bounds.append(up(at, 2))

    def fetch(k):
        for q in range(cuts[k], min(cuts[k + 1], whole)):
            pltpu.make_async_copy(
                x_hbm.at[0, :, pl.ds(q * chunk, chunk)],
                lhs_ref.at[pl.ds(chunk_at[q] * rows, rows), :],
                sems.at[len(small) + k],
            ).start()

    rest = pltpu.make_async_copy(
        x_hbm.at[0, :, pl.ds(whole * chunk, total - whole * chunk)], tail_ref, sems.at[len(small) + stages]
    )
    fetch(0)
    for each in small:
        each.wait()
    for k in range(1, stages):
        fetch(k)
    rest.start()

    period = math.lcm(SUB, factor)
    middle = LANES // 2
    taps = jnp.concatenate([taps_ref[...].astype(F32), jnp.zeros((1, LANES - tap_count), F32)], axis=1)
    taps = jnp.broadcast_to(taps, (SUB, LANES))
    lane8 = iota((SUB, LANES), 1)
    seeds = []
    for start in range(0, period, SUB):
        tap = factor * (lane8 - middle) + (factor - 1 - start) - iota((SUB, LANES), 0)
        tap = jnp.where((tap >= 0) & (tap < tap_count), tap, LANES - 1)
        seeds.append(jnp.take_along_axis(taps, tap, axis=1, mode="promise_in_bounds"))
    nothing = jnp.zeros((SUB, LANES), F32)
    for row in range(0, chunk, 2 * SUB):
        inside, beyond = [], []
        for start in (row, row + SUB):
            moved = start // period * (period // factor)
            block = pltpu.roll(seeds[start % period // SUB], (moved - middle) % LANES, 1)
            last = moved > LANES - 2 * SUB
            inside.append(jnp.where(lane8 >= middle, block, 0.0) if last else block)
            beyond.append(jnp.where(lane8 < middle, block, 0.0) if last else nothing)
        band_ref[row : row + 2 * SUB, :LANES] = jnp.concatenate(inside, axis=0).astype(BF16)
        band_ref[row : row + 2 * SUB, LANES:] = jnp.concatenate(beyond, axis=0).astype(BF16)

    own = lax.axis_index("freq")
    bin_count = bins_ref.shape[1]
    held = up(bin_count, LANES)
    bins = bins_ref[...]
    if held > bin_count:
        bins = jnp.concatenate([bins, jnp.zeros((1, held - bin_count), jnp.int32)], axis=1)
    bins = jnp.broadcast_to(bins, (SUB, held))
    lane = iota((SUB, 2 * half), 1)
    is_imag = lane >= half
    valid = (lane & (half - 1)) < per_group
    blocks = up(length, 2 * LANES) // LANES
    pairs = blocks // 2
    row8 = iota((SUB, 2 * half), 0)
    table_parts = []
    for slot in range(groups):
        first = lax.rem(own + slot, groups) * per_group
        real = pltpu.roll(bins, lax.rem(held - first, held), 1)[:, : 2 * half]
        imag = pltpu.roll(bins, lax.rem(held - first + half, held), 1)[:, : 2 * half]
        bins8 = jnp.where(is_imag, imag, real)
        c, s = cos_sin(wrap((row8 + (blocks - 1) * LANES // 2) * bins8, length), length)
        near = jnp.where(valid, jnp.where(is_imag, -s, c), 0.0), jnp.where(valid, jnp.where(is_imag, -c, -s), 0.0)
        rise = [cos_sin(wrap((row8 + r) * SUB * bins8, length), length) for r in range(0, LANES // SUB, SUB)]
        apart = [cos_sin(wrap((2 * (row8 + r) + 1) * (LANES // 2) * bins8, length), length) for r in range(0, pairs, SUB)]
        table_parts.append((near, rise, apart))

    def table_rows(slot, row):
        (near_v, near_w), rise, apart = table_parts[slot]
        here = []
        for start in (row // SUB, row // SUB + 1):
            turn_c, turn_s = (t[start % SUB : start % SUB + 1] for t in rise[start // SUB])
            here.append((near_v * turn_c + near_w * turn_s, near_w * turn_c - near_v * turn_s))
        here = [jnp.concatenate(h, axis=0) for h in zip(*here)]
        for d in range(pairs):
            turn_c, turn_s = (t[d % SUB : d % SUB + 1] for t in apart[d // SUB])
            even, odd = here[0] * turn_c, here[1] * turn_s
            for block, value in ((pairs + d, even + odd), (pairs - 1 - d, even - odd)):
                table_ref[
                    block * LANES + row : block * LANES + row + 2 * SUB,
                    slot * 2 * half : (slot + 1) * 2 * half,
                ] = value.astype(BF16)

    todo = [(slot, row) for slot in range(groups) for row in range(0, LANES, 2 * SUB)]

    def land(k):
        landed = lhs_ref.at[copied[k], :]
        pltpu.make_async_copy(landed, landed, sems.at[len(small) + k]).wait()
        end = bounds[k] + cuts[k + 1] - cuts[k]
        if cuts[k + 1] > whole:
            rest.wait()
            tail = tail_ref[...].astype(F32)
            tail = jnp.concatenate([tail, jnp.zeros((rows, chunk - tail.shape[1]), F32)], axis=1)
            lhs_ref[(end - 1) * rows : end * rows, :] = tail.astype(BF16)
        for w, at in first_at.items():
            if not bounds[k] <= at < bounds[k + 1]:
                continue
            begin = w * length * factor
            source, lead = chunk_at[begin // chunk] * rows, begin % chunk
            whole_row = lhs_ref[source : source + rows, :].astype(F32)
            kept = jnp.where(iota(whole_row.shape, 1) >= lead, whole_row, 0.0)
            lhs_ref[at * rows : (at + 1) * rows, :] = kept.astype(BF16)
            end += 1
        if end < bounds[k + 1]:
            lhs_ref[end * rows : bounds[k + 1] * rows, :] = jnp.zeros(((bounds[k + 1] - end) * rows, chunk), BF16)

    def decimate(k):
        middle_at = bounds[k] + up((bounds[k + 1] - bounds[k]) // 2, 2)
        for begin, end in ((bounds[k], middle_at), (middle_at, bounds[k + 1])):
            span = slice(begin * rows, end * rows)
            got = jnp.dot(lhs_ref[span, :], band_ref[...], preferred_element_type=F32)
            dec_ref[span, :] = got[:, :LANES]
            carry_ref[span, :] = got[:, LANES:]

    zero_tile = jnp.zeros((rows, LANES), F32)

    def dec(q, w=None):
        at = chunk_at[q] if w is None else first_at[w]
        got = dec_ref[at * rows : (at + 1) * rows, :]
        if q and w is None:
            at = chunk_at[q - 1]
            got = got + carry_ref[at * rows : (at + 1) * rows, :]
        return got

    def window_rows(w):
        first, lead = divmod(w * length, LANES)
        span = -(-(length + lead) // LANES)
        turned = [dec(first, w if w and lead else None)] + [dec(first + n) for n in range(1, span)]
        if lead:
            turned = [pltpu.roll(t, LANES - lead, 1) for t in turned]
        found = []
        for block in range(blocks):
            left = length - block * LANES
            if left <= 0:
                found.append(zero_tile)
                continue
            low = turned[block]
            if lead and block + 1 < span:
                low = jnp.where(lane8 < LANES - lead, low, turned[block + 1])
            found.append(jnp.where(lane8 < left, low, 0.0) if left < LANES else low)
        return found

    def window_pair(w):
        for block, pair in enumerate(zip(window_rows(w), window_rows(w + 1))):
            rows_ref[w * rows : (w + 2) * rows, block * LANES : (block + 1) * LANES] = (
                jnp.concatenate(pair, axis=0).astype(BF16)
            )

    waiting = list(range(0, windows, 2))

    def ready_windows(chunks_done):
        while waiting and -(-(waiting[0] + 2) * length // LANES) <= chunks_done:
            window_pair(waiting.pop(0))

    share = -(-len(todo) // (stages + 1))
    for slot, row in todo[:share]:
        table_rows(slot, row)
    for k in range(stages):
        land(k)
        decimate(k)
        for slot, row in todo[(k + 1) * share : (k + 2) * share]:
            table_rows(slot, row)
        ready_windows(cuts[k + 1])
    spectrum = jnp.dot(rows_ref[...], table_ref[...], preferred_element_type=F32)
    power = jnp.sum(spectrum * spectrum, axis=1, keepdims=True) / bin_count
    row = iota((windows * rows, 1), 0) & (rows - 1)
    live = jnp.zeros((windows * rows, 1), F32)
    for r in range(rows):
        live = jnp.where(row == r, mask_ref[0, r].astype(F32), live)
    scale = lax.rsqrt(power + 1e-06) * live
    for slot in range(groups):
        piece = spectrum[:, slot * 2 * half : (slot + 1) * 2 * half] * scale
        outs[slot][...] = piece.astype(BF16)


def front(raw_strain, fir_taps, band_bins, live_mask, groups):
    rows = raw_strain.shape[1]
    bins = band_bins.shape[0]
    per_group = bins // groups
    half = up(per_group, 64)
    dims = (WIN, NT, DECIM, groups, per_group, half, rows)
    width = groups * 2 * half
    total = raw_strain.shape[2]
    chunks = -(-total // (DECIM * LANES))
    stages = 4
    entries = chunks + WIN - 1 + 2 * stages
    blocks = up(NT, 2 * LANES)
    vmem = pl.BlockSpec(memory_space=pltpu.VMEM)
    return pl.pallas_call(
        functools.partial(front_kernel, dims),
        out_shape=[jax.ShapeDtypeStruct((WIN * rows, 2 * half), BF16)] * groups,
        in_specs=[pl.BlockSpec(memory_space=pltpu.HBM)] * 4,
        out_specs=[vmem] * groups,
        scratch_shapes=[
            pltpu.VMEM((rows, total % (DECIM * LANES)), BF16),
            pltpu.SMEM(live_mask.shape, jnp.int32),
            pltpu.VMEM((1, fir_taps.shape[0]), BF16),
            pltpu.VMEM((1, bins), jnp.int32),
            pltpu.VMEM((DECIM * LANES, 2 * LANES), BF16),
            pltpu.VMEM((blocks, width), BF16),
            pltpu.VMEM((up(entries, 2) * rows, DECIM * LANES), BF16),
            pltpu.VMEM((up(entries, 2) * rows, LANES), F32),
            pltpu.VMEM((up(entries, 2) * rows, LANES), F32),
            pltpu.VMEM((WIN * rows, blocks), BF16),
            pltpu.SemaphoreType.DMA((4 + stages,)),
        ],
        compiler_params=pltpu.CompilerParams(vmem_limit_bytes=20 << 20),
        name="front",
    )(*[
        pltpu.with_memory_space_constraint(a, pltpu.HBM)
        for a in (live_mask, raw_strain, fir_taps[None, :], band_bins[None, :])
    ])


def rows_kernel(dims, parts_ref, out_ref, turned_ref):
    windows, rows, zs, half, per_group, pack = dims
    height = rows * zs
    own = lax.axis_index("freq")
    lane = iota((height, 2 * half), 1)
    depth = 2 * windows
    blank = jnp.zeros((LANES - 2 * height, 2 * half), F32)
    for pair in range(0, windows, 2):
        mine = ([], [])
        for z in range(zs):
            slot = lax.rem(own + zs - z, zs)
            got = parts_ref[slot, pair * rows : (pair + 2) * rows, :].astype(F32)
            mine[0].append(got[:rows])
            mine[1].append(got[rows:])
        for e in range(2):
            straight = jnp.concatenate(mine[e], axis=0)
            swapped = pltpu.roll(straight, half, 1)
            swapped = jnp.where(lane < half, swapped, -swapped)
            flipped = jnp.concatenate([straight, swapped, blank], axis=0).T
            for part in range(2):
                turned_ref[pl.ds(2 * (pair + e) + part, half, stride=depth), :] = flipped[part * half : (part + 1) * half]
    lane = iota((2 * height, LANES), 1)
    for group in range(per_group // pack):
        got = turned_ref[group * pack * depth : (group + 1) * pack * depth, :]
        got = jnp.concatenate([got, jnp.zeros((LANES - pack * depth, LANES), F32)], axis=0).T[: 2 * height]
        for k in range(pack):
            inside = (lane >= k * depth) & (lane < (k + 1) * depth)
            out_ref[group, k * 2 * height : (k + 1) * 2 * height, :] = jnp.where(inside, got, 0.0).astype(BF16)


def correlate_kernel(dims, left_ref, parts_ref, out_hbm, *refs):
    windows, rows, zs, blocks, half, per_group, pack = dims
    *spec_refs, out_ref, sems = refs
    height = rows * zs
    depth = 2 * windows
    block = lax.axis_index("chan")
    own = lax.axis_index("freq")
    per_tile = LANES // height
    for pair in range(0, windows, 2):
        for tile, spec_ref in enumerate(spec_refs):
            slabs = ([], [])
            for b in range(tile * per_tile, (tile + 1) * per_tile):
                for z in range(zs):
                    slot = lax.rem(own + zs - z, zs)
                    got = parts_ref[(block ^ b) & 1, (block ^ b) >> 1, slot, pair * rows : (pair + 2) * rows, :].astype(F32)
                    slabs[0].append(got[:rows])
                    slabs[1].append(got[rows:])
            for e in range(2):
                flipped = jnp.concatenate(slabs[e], axis=0).T
                for part in range(2):
                    spec_ref[pl.ds(2 * (pair + e) + part, half, stride=depth), :] = flipped[part * half : (part + 1) * half]
    copies = []
    for group in range(per_group // pack):
        at = group * pack * depth
        right = [ref[at : at + pack * depth, :] for ref in spec_refs]
        right = jnp.concatenate(right, axis=1).astype(BF16)
        prod = jnp.dot(left_ref[group, :, : pack * depth], right, preferred_element_type=F32)
        prod = prod * F32(1.0 / windows)
        first = group * pack
        out_ref[first : first + pack] = prod.reshape(pack, 2, height, prod.shape[1])
        copies.append(pltpu.make_async_copy(out_ref.at[pl.ds(first, pack)], out_hbm.at[pl.ds(first, pack)], sems.at[group]))
        copies[-1].start()
    for each in copies:
        each.wait()


def pack_of(per_group, windows):
    return next(p for p in (4, 2, 1) if per_group % p == 0 and 2 * windows * p <= LANES)


def row_side(parts, per_group, rows):
    zs, full_rows, lanes = parts.shape
    windows = full_rows // rows
    pack = pack_of(per_group, windows)
    half = lanes // 2
    height = rows * zs
    vmem = pl.BlockSpec(memory_space=pltpu.VMEM)
    return pl.pallas_call(
        functools.partial(rows_kernel, (windows, rows, zs, half, per_group, pack)),
        out_shape=jax.ShapeDtypeStruct((per_group // pack, pack * 2 * height, LANES), BF16),
        in_specs=[vmem],
        out_specs=vmem,
        scratch_shapes=[pltpu.VMEM((half * 2 * windows, LANES), F32)],
        compiler_params=pltpu.CompilerParams(vmem_limit_bytes=8 << 20),
        cost_estimate=pl.CostEstimate(flops=1 << 24, bytes_accessed=4 << 20, transcendentals=0),
        name="rows",
    )(parts)


def correlate(left, parts, per_group, rows):
    _, chips, zs, full_rows, lanes = parts.shape
    blocks = 2 * chips
    windows = full_rows // rows
    half = lanes // 2
    height = rows * zs
    width = height * blocks
    pack = pack_of(per_group, windows)
    dims = (windows, rows, zs, blocks, half, per_group, pack)
    vmem = pl.BlockSpec(memory_space=pltpu.VMEM)
    shape = (per_group, 2, height, width)
    return pl.pallas_call(
        functools.partial(correlate_kernel, dims),
        out_shape=jax.ShapeDtypeStruct(shape, F32),
        in_specs=[vmem, vmem],
        out_specs=pl.BlockSpec(memory_space=pltpu.HBM),
        scratch_shapes=[pltpu.VMEM((half * 2 * windows, LANES), F32)] * (width // LANES)
        + [pltpu.VMEM(shape, F32), pltpu.SemaphoreType.DMA((per_group // pack,))],
        compiler_params=pltpu.CompilerParams(vmem_limit_bytes=(24 if blocks <= 8 else 44) << 20),
        name="correlate",
    )(left, parts)


def shards(groups, blocks, raw_strain, fir_taps, band_bins, live_mask):
    rows = raw_strain.shape[1]
    per_group = band_bins.shape[0] // groups
    pieces = front(raw_strain, fir_taps, band_bins, live_mask, groups)
    got = [pieces[0]]
    for slot in range(1, groups):
        pairs = [(i, (i + slot) % groups) for i in range(groups)]
        got.append(lax.ppermute(pieces[slot], "freq", pairs))
    parts = jnp.stack(got)
    left = row_side(parts, per_group, rows)
    same = [parts[None]]
    for step in range(2, blocks, 2):
        same.append(lax.ppermute(parts[None], "chan", [(i, i ^ step) for i in range(blocks)]))
    same = jnp.concatenate(same, axis=0)
    other = lax.ppermute(same, "chan", [(i, i ^ 1) for i in range(blocks)])
    both = jnp.stack([same, other])
    return correlate(left, both, per_group, rows)


def solution(mesh):
    in_specs = (P("chan", "freq", None), P(), P(), P("chan", "freq"))
    out_specs = P("freq", None, "chan", None)
    body = functools.partial(shards, mesh.shape["freq"], mesh.shape["chan"])
    return jax.shard_map(body, mesh=mesh, in_specs=in_specs, out_specs=out_specs, check_vma=False)
```
